1024 devices in a mesh: pair: 2 (over y_lo), section: 16 (over z), dp: 32 (over y_hi, x, core).
Axes of the slice: x: 4, y: 8 (y_hi: 4, y_lo: 2; y = y_hi * 2 + y_lo), z: 16, core: 2. Of those that a mesh axis runs over, the one named last changes fastest.
Arguments:
- grads: float32 [32, 32, 64, 7168], P(('section', 'pair'), 'dp'), parts along dimension 0, may hold values from -6 to 6
- master: float32 [1024, 7168], P(('section', 'pair', 'dp')), parts along dimension 0, may hold values from -6 to 6
- moment: float32 [1024, 7168], P(('section', 'pair', 'dp')), parts along dimension 0, may hold values from -12 to 12
- second: float32 [1024, 7168], P(('section', 'pair', 'dp')), parts along dimension 0, may hold values from 0.5 to 50
- step: int32 [16], P('section'), parts along dimension 0, may hold values from 1 to 8
Outputs:
- new_master: float32 [1024, 7168], P(('section', 'pair', 'dp')), parts along dimension 0
- new_moment: float32 [1024, 7168], P(('section', 'pair', 'dp')), parts along dimension 0
- new_second: float32 [1024, 7168], P(('section', 'pair', 'dp')), parts along dimension 0
- params: bfloat16 [1024, 7168], P('section'), parts along dimension 0
The draws below stay inside these ranges and needn't reach their ends.
There are 16 independent parts, one for each index of `section`. The reference program is written for one: setup_inputs(seed, part) draws one part's arguments, and reference() takes and returns one part's arrays. A program takes and returns all parts, laid end to end along the dimension named above; each array names one. Nothing has to cross between parts.
All inputs are finite; a program needn't handle non-finite values.
Results may differ from the reference program's by a relative error of at most 0.0004.
Values may be sent and summed in bfloat16 or wider, within the bound.
A program may use at most 32 MiB of HBM per device.

```python
import math
import jax
import jax.numpy as jnp
from jax import lax

D = 7168
ROWS = 64
N_PAIR = 2
N_DP = 32


def spiked(drawn, key, source, target, blocks, factor):
    owner, partner = [(jnp.arange(drawn.shape[dim]) // (drawn.shape[dim] // blocks)).reshape([-1 if axis == dim else 1 for axis in range(drawn.ndim)]) for dim in (source, target)]
    chosen = jax.random.permutation(key, blocks)[partner]
    strong = (owner == chosen) | (owner == (partner + blocks // 2) % blocks)
    return jnp.where(strong, factor * drawn, drawn)


def shard_levels(key, extent, shards, low, largest):
    loudness = 1.0
    for position, parts in shards:
        heights = jax.random.uniform(jax.random.fold_in(jax.random.fold_in(key, 6), position), (parts,), jnp.float32, low / len(shards), largest / len(shards))
        loudness = loudness * jnp.repeat(jnp.exp(heights), extent[position] // parts).reshape((-1,) + (1,) * (len(extent) - 1 - position))
    return loudness


def gaussian(stream_key, extent, scale, reach, cuts=(), held_as=jnp.bfloat16):
    factor_of = shard_levels(stream_key, extent, cuts, -0.22, 0.18) if cuts else 1.0
    array = jax.random.normal(stream_key, extent, jnp.float32) * scale * factor_of
    return jnp.minimum(jnp.maximum(array, -reach), reach).astype(held_as)


def bell_draw_with(key, extent, width, bound, split, heavy, kind=jnp.bfloat16):
    array = width * jax.random.normal(key, extent, jnp.float32)
    if split:
        array = array * shard_levels(key, extent, split, -0.22, 0.18)
    return jnp.clip(spiked(array, jax.random.fold_in(key, 3), *heavy), -bound, bound).astype(kind)


def setup_inputs(seed: int = 0, part: int = 0) -> dict:
    seeds = jax.random.split(jax.random.key(seed), 6)
    part_keys = jax.random.split(jax.random.fold_in(seeds[5], part), 6)
    grads = bell_draw_with(part_keys[0], (N_PAIR, N_DP, ROWS, D), 1.0, 6.0, ((0, 2), (1, 32)), (1, 2, 32, 2.75), jnp.float32)
    master = gaussian(part_keys[1], (ROWS, D), 1.0, 6.0, ((0, 64),), jnp.float32)
    moment = gaussian(part_keys[2], (ROWS, D), 2.0, 12.0, ((0, 64),), jnp.float32)
    second = jnp.clip(jnp.exp(math.log(50.0) - 4.6051702 * jax.random.uniform(part_keys[3], (ROWS, D), jnp.float32) ** shard_levels(part_keys[3], (ROWS, D), ((0, 64),), -0.2, 0.2)), 0.5, 50.0)
    step = jax.random.randint(part_keys[4], (1,), 1, 9).astype(jnp.int32)
    return dict(grads=grads, master=master, moment=moment, second=second, step=step)


def reference(grads, master, moment, second, step):
    total = lax.optimization_barrier(jnp.sum(grads.astype(jnp.float32), axis=(0, 1)))
    new_moment = 0.9 * moment + 0.1 * total
    new_second = 0.95 * second + 0.05 * total * total
    count = step[0].astype(jnp.float32)
    first_fix = 1.0 - jnp.power(jnp.float32(0.9), count)
    second_fix = 1.0 - jnp.power(jnp.float32(0.95), count)
    update = new_moment / first_fix / (jnp.sqrt(new_second / second_fix) + 1e-08) + 0.1 * master
    new_master = master - 0.03 * update
    return (new_master, new_moment, new_second, new_master.astype(jnp.bfloat16))
```

```python
import functools

import jax
import jax.numpy as jnp
from jax import lax
from jax.experimental import pallas as pl
from jax.experimental.pallas import tpu as pltpu
from jax.sharding import PartitionSpec as P

MESH = pl.DeviceIdType.MESH
F32 = jnp.float32
BF16 = jnp.bfloat16
J = 56


def kernel(
    step_ref, g_ref, master_ref, moment_ref, second_ref,
    new_master_ref, new_moment_ref, new_second_ref, params_ref,
    mine, sib, xs, t3, t4, rm1, rm2, r3, r4, ys, yr, rows, wide,
    load_sem, d_send, d_recv, x_send, x_recv, y_send, y_recv,
    ay_send, a_recv, ax_send, ad_send,
):
    ylo = lax.axis_index("pair")
    dp = lax.axis_index("dp")
    c = lax.rem(dp, 2)
    x = lax.rem(dp // 2, 4)
    yhi = dp // 8
    y = yhi * 2 + ylo
    oc = 1 - c
    xp = lax.rem(x + 1, 4)
    xm = lax.rem(x + 3, 4)
    xo = lax.rem(x + 2, 4)

    def dev(lo, hi, xx, cc):
        return {"pair": lo, "dp": (hi * 4 + xx) * 2 + cc}

    sibling = dev(ylo, yhi, x, oc)
    plus = dev(ylo, yhi, xp, c)
    minus = dev(ylo, yhi, xm, c)

    def remote(src, dst, ssem, rsem, where):
        return pltpu.make_async_remote_copy(
            src_ref=src, dst_ref=dst, send_sem=ssem, recv_sem=rsem,
            device_id=where, device_id_type=MESH,
        )

    hi_of = [lax.rem(yhi + 2 + k, 4) for k in range(4)]

    loads = []
    for k in range(4):
        cp = pltpu.make_async_copy(g_ref.at[c * 4 + hi_of[k]], mine.at[k], load_sem.at[k])
        cp.start()
        loads.append(cp)

    barrier = pltpu.get_barrier_semaphore()
    for where in (sibling, plus, minus):
        pl.semaphore_signal(barrier, inc=1, device_id=where, device_id_type=MESH)
    for d in range(1, 8):
        yy = lax.rem(y + d, 8)
        for cc in range(2):
            pl.semaphore_signal(
                barrier, inc=1, device_id=dev(lax.rem(yy, 2), yy // 2, x, cc), device_id_type=MESH
            )
    pl.semaphore_wait(barrier, 17)

    d_copies = []
    for k in range(4):
        cp = remote(g_ref.at[oc * 4 + hi_of[k]], sib.at[k], d_send.at[k], d_recv.at[k], sibling)
        cp.start()
        d_copies.append(cp)

    pending = []

    def send(*args):
        cp = remote(*args)
        cp.start()
        pending.append(cp)
        return cp

    m1, m2, m3, m4 = {}, {}, {}, {}

    def stage_sum(k):
        loads[k].wait()
        d_copies[k].wait_recv()
        a = mine.at[k].reshape(J * 8, 128)
        b = sib.at[k].reshape(J * 8, 128)
        for s in range(8):
            for jb in range(7):
                sl = pl.ds(jb * 64 + s, 8, stride=8)
                xs[s // 2, k, s % 2, pl.ds(jb * 8, 8), :] = a[sl, :] + b[sl, :]
        m1[k] = send(xs.at[xo, k, 0], rm1.at[k], x_send.at[0, k], x_recv.at[0, k], plus)
        m2[k] = send(xs.at[xo, k, 1], rm2.at[k], x_send.at[1, k], x_recv.at[1, k], minus)
        m3[k, 1] = send(xs.at[xp, k, 1], r3.at[k, 1], x_send.at[2, k], x_recv.at[2, k], plus)
        m4[k, 0] = send(xs.at[xm, k, 0], r4.at[k, 0], x_send.at[3, k], x_recv.at[3, k], minus)

    def stage_relay(k):
        m1[k].wait_recv()
        t3[k] = xs[xp, k, 0] + rm1[k]
        m3[k, 0] = send(t3.at[k], r3.at[k, 0], x_send.at[4, k], x_recv.at[4, k], plus)
        m2[k].wait_recv()
        t4[k] = xs[xm, k, 1] + rm2[k]
        m4[k, 1] = send(t4.at[k], r4.at[k, 1], x_send.at[5, k], x_recv.at[5, k], minus)

    def stage_y(k):
        hi = hi_of[k]
        for cc in range(2):
            m3[k, cc].wait_recv()
            m4[k, cc].wait_recv()
            ys[k, cc] = xs[x, k, cc] + r3[k, cc] + r4[k, cc]
            if k == 2:
                own = jnp.logical_and(c == ylo, c == cc)

                @pl.when(own)
                def _():
                    yr[y] = ys[k, cc]

                @pl.when(jnp.logical_not(own))
                def _():
                    remote(ys.at[k, cc], yr.at[y], y_send.at[k, cc], y_recv.at[y], dev(c, hi, x, cc)).start()
            else:
                remote(ys.at[k, cc], yr.at[y], y_send.at[k, cc], y_recv.at[y], dev(c, hi, x, cc)).start()

    stage_sum(0)
    stage_sum(1)
    stage_relay(0)
    stage_sum(2)
    stage_relay(1)
    stage_sum(3)
    stage_relay(2)
    stage_y(0)
    stage_relay(3)
    stage_y(1)
    stage_y(2)
    stage_y(3)

    def y_wait(slot):
        remote(ys.at[0, 0], yr.at[slot], y_send.at[0, 0], y_recv.at[slot], sibling).wait_recv()

    @pl.when(c != ylo)
    def _():
        y_wait(y)

    for d in (1, 7, 2, 6, 3, 5, 4):
        y_wait(lax.rem(y + d, 8))
    total = yr[0]
    for i in range(1, 8):
        total = total + yr[i]

    t = step_ref[0]
    p1 = jnp.float32(1.0)
    p2 = jnp.float32(1.0)
    b1, b2 = 0.9, 0.95
    for bit in range(8):
        on = lax.rem(lax.shift_right_logical(t, bit), 2) == 1
        p1 = p1 * jnp.where(on, jnp.float32(b1), jnp.float32(1.0))
        p2 = p2 * jnp.where(on, jnp.float32(b2), jnp.float32(1.0))
        b1, b2 = b1 * b1, b2 * b2
    first_fix = 1.0 - p1
    second_fix = 1.0 - p2
    master = master_ref[...]
    new_moment = 0.9 * moment_ref[...] + 0.1 * total
    new_second = 0.95 * second_ref[...] + 0.05 * total * total
    ff = jnp.full((J, 128), first_fix, F32)
    sf = jnp.full((J, 128), second_fix, F32)
    update = new_moment / ff / (jnp.sqrt(new_second / sf) + 1e-08) + 0.1 * master
    new_master = master - 0.03 * update
    new_master_ref[...] = new_master
    new_moment_ref[...] = new_moment
    new_second_ref[...] = new_second

    def row_of(yy, xx, cc):
        return lax.rem(yy, 2) * 32 + (yy // 2) * 8 + xx * 2 + cc

    rows[row_of(y, x, c)] = new_master.astype(BF16)

    def pass_on(r, sems, where):
        send(rows.at[r], rows.at[r], sems, a_recv.at[r], where)

    def arrive(r):
        remote(rows.at[r], rows.at[r], ad_send.at[0], a_recv.at[r], sibling).wait_recv()

    me = row_of(y, x, c)
    for i, d in enumerate((4, 3, 5, 2, 6, 1, 7)):
        yy = lax.rem(y + d, 8)
        pass_on(me, ay_send.at[i], dev(lax.rem(yy, 2), yy // 2, x, c))
    far = (0, 1, 7, 2, 6, 3, 5, 4)

    def spread(i):
        yy = lax.rem(y + far[i], 8)
        r = row_of(yy, x, c)
        if i:
            arrive(r)
        pass_on(r, ax_send.at[0, i], plus)
        pass_on(r, ax_send.at[1, i], minus)
        pass_on(r, ad_send.at[i], sibling)

    def relay(i):
        yy = lax.rem(y + far[i], 8)
        rm_ = row_of(yy, xm, c)
        rp_ = row_of(yy, xp, c)
        arrive(rm_)
        if i % 2 == 0:
            pass_on(rm_, ax_send.at[2, i], plus)
        pass_on(rm_, ad_send.at[8 + i], sibling)
        arrive(rp_)
        if i % 2 == 1:
            pass_on(rp_, ax_send.at[2, i], minus)
        pass_on(rp_, ad_send.at[16 + i], sibling)

    def last(i):
        yy = lax.rem(y + far[i], 8)
        r = row_of(yy, xo, c)
        arrive(r)
        pass_on(r, ad_send.at[24 + i], sibling)

    for i in range(8):
        spread(i)
    for i in range(8):
        relay(i)
    for i in range(8):
        last(i)
    for yy in range(8):
        for xx in range(4):
            arrive(row_of(yy, xx, oc))

    for gp in range(4):
        for s in range(16):
            wide[s] = rows[gp * 16 + s].astype(F32)
        w = wide.reshape(16 * J, 128)
        for j in range(J):
            params_ref[pl.ds(gp * 16, 16), pl.ds(j * 128, 128)] = w[pl.ds(j, 16, stride=J), :].astype(BF16)

    for cp in d_copies:
        cp.wait_send()
    for cp in pending:
        cp.wait_send()
    for k in range(4):
        for cc in range(2):
            def done():
                remote(ys.at[k, cc], yr.at[0], y_send.at[k, cc], y_recv.at[0], sibling).wait_send()

            if k == 2:
                pl.when(jnp.logical_not(jnp.logical_and(c == ylo, c == cc)))(done)
            else:
                done()


def per_device(grads, master, moment, second, step):
    g = grads.reshape(8, 8, J, 128).transpose(0, 2, 1, 3)
    row = jax.ShapeDtypeStruct((J, 128), F32)
    vmem = pl.BlockSpec(memory_space=pltpu.VMEM)
    dma = pltpu.SemaphoreType.DMA
    outs = pl.pallas_call(
        kernel,
        out_shape=(row, row, row, jax.ShapeDtypeStruct((64, J * 128), BF16)),
        in_specs=[pl.BlockSpec(memory_space=pltpu.SMEM), pl.BlockSpec(memory_space=pl.ANY), vmem, vmem, vmem],
        out_specs=(vmem, vmem, vmem, vmem),
        scratch_shapes=[
            pltpu.VMEM((4, J, 8, 128), F32),
            pltpu.VMEM((4, J, 8, 128), F32),
            pltpu.VMEM((4, 4, 2, J, 128), F32),
            pltpu.VMEM((4, J, 128), F32),
            pltpu.VMEM((4, J, 128), F32),
            pltpu.VMEM((4, J, 128), F32),
            pltpu.VMEM((4, J, 128), F32),
            pltpu.VMEM((4, 2, J, 128), F32),
            pltpu.VMEM((4, 2, J, 128), F32),
            pltpu.VMEM((4, 2, J, 128), F32),
            pltpu.VMEM((8, J, 128), F32),
            pltpu.VMEM((64, J, 128), BF16),
            pltpu.VMEM((16, J, 128), F32),
            dma((4,)), dma((4,)), dma((4,)),
            dma((6, 4)), dma((6, 4)),
            dma((4, 2)), dma((8,)),
            dma((7,)), dma((64,)), dma((3, 8)), dma((32,)),
        ],
        compiler_params=pltpu.CompilerParams(collective_id=0, has_side_effects=True),
    )(step, g, master.reshape(J, 128), moment.reshape(J, 128), second.reshape(J, 128))
    new_master, new_moment, new_second, params = outs
    flat = (1, J * 128)
    return (new_master.reshape(flat), new_moment.reshape(flat), new_second.reshape(flat), params)


def solution(mesh):
    placed = (
        P(("section", "pair"), "dp", None, None),
        P(("section", "pair", "dp"), None),
        P(("section", "pair", "dp"), None),
        P(("section", "pair", "dp"), None),
        P("section"),
    )
    return jax.shard_map(
        per_device,
        mesh=mesh,
        in_specs=placed,
        out_specs=(
            P(("section", "pair", "dp"), None),
            P(("section", "pair", "dp"), None),
            P(("section", "pair", "dp"), None),
            P("section", None),
        ),
        check_vma=False,
    )
```

```python
import jax
import jax.numpy as jnp
from jax import lax
from jax.experimental import pallas as pl
from jax.experimental.pallas import tpu as pltpu
from jax.sharding import PartitionSpec as P

MESH = pl.DeviceIdType.MESH
F32 = jnp.float32
BF16 = jnp.bfloat16
I16 = jnp.int16
J = 56
CODE = 64
TOP = 32700.0
STEPS = 256.0
FAR = (1, 7, 2, 6, 3, 5, 4)


def encode(v):
    v = v.reshape(7, 8, 128)
    largest = jnp.maximum(jnp.max(jnp.abs(v), axis=0), 1e-30)
    e = jnp.ceil(jnp.log2(largest) * STEPS)
    q = jnp.round(v * (TOP * jnp.exp2(e * (-1.0 / STEPS)))[None])
    return jnp.concatenate([q.reshape(J, 128), e], axis=0).astype(jnp.int32).astype(I16)


def decode(code):
    f = code.astype(jnp.int32).astype(F32)
    scale = jnp.exp2(f[J:] * (1.0 / STEPS)) * (1.0 / TOP)
    return (f[:J].reshape(7, 8, 128) * scale[None]).reshape(J, 128)


def reduce_update_gather(
    step_hbm, g_ref, master_hbm, moment_hbm, second_hbm,
    new_master_ref, new_moment_ref, new_second_ref, rows,
    mine, sib, xs, xcode, xin, ycode, yin, state, step_ref,
    load_sem, state_sem, d_send, d_recv, x_send, x_recv, y_send, y_recv,
    ay_send, a_recv, ax_send, ad_send,
):
    ylo = lax.axis_index("pair")
    dp = lax.axis_index("dp")
    c = lax.rem(dp, 2)
    x = lax.rem(dp // 2, 4)
    yhi = dp // 8
    y = yhi * 2 + ylo
    oc = 1 - c
    xp = lax.rem(x + 1, 4)
    xm = lax.rem(x + 3, 4)
    xo = lax.rem(x + 2, 4)

    def dev(yy, xx, cc):
        return {"pair": lax.rem(yy, 2), "dp": ((yy // 2) * 4 + xx) * 2 + cc}

    sibling = dev(y, x, oc)
    across = [dev(y, xx, c) for xx in (xo, xp, xm)]

    def remote(src, dst, ssem, rsem, where):
        return pltpu.make_async_remote_copy(
            src_ref=src, dst_ref=dst, send_sem=ssem, recv_sem=rsem,
            device_id=where, device_id_type=MESH,
        )

    barrier = pltpu.get_barrier_semaphore()
    for where in [sibling] + across:
        pl.semaphore_signal(barrier, inc=1, device_id=where, device_id_type=MESH)
    for d in FAR:
        yy = lax.rem(y + d, 8)
        for cc in range(2):
            pl.semaphore_signal(barrier, inc=1, device_id=dev(yy, x, cc), device_id_type=MESH)

    hi_of = [lax.rem(yhi + d, 4) for d in (2, 1, 3, 0)]
    loads = []
    for k in range(4):
        cp = pltpu.make_async_copy(g_ref.at[c * 4 + hi_of[k]], mine.at[k], load_sem.at[k])
        cp.start()
        loads.append(cp)
    state_copies = [
        pltpu.make_async_copy(src, dst, state_sem.at[i])
        for i, (src, dst) in enumerate((
            (step_hbm, step_ref), (master_hbm, state.at[0]), (moment_hbm, state.at[1]), (second_hbm, state.at[2]),
        ))
    ]
    for cp in state_copies:
        cp.start()

    pl.semaphore_wait(barrier, 18)

    pending = []

    def send(*args):
        cp = remote(*args)
        cp.start()
        pending.append(cp)
        return cp

    d_copies = [
        send(g_ref.at[oc * 4 + hi_of[k]], sib.at[k], d_send.at[k], d_recv.at[k], sibling) for k in range(4)
    ]
    x_copies = {}

    def stage_sum(k):
        loads[k].wait()
        d_copies[k].wait_recv()
        a = mine.at[k].reshape(J * 8, 128)
        b = sib.at[k].reshape(J * 8, 128)

        def summed(xx, cc):
            pieces = []
            for jb in range(7):
                sl = pl.ds(jb * 64 + xx * 2 + cc, 8, stride=8)
                pieces.append(a[sl, :] + b[sl, :])
            return jnp.concatenate(pieces, axis=0)

        for i, xx in enumerate((xo, xp, xm)):
            for cc in range(2):
                xcode[k, i, cc] = encode(summed(xx, cc))
            x_copies[k, i] = send(xcode.at[k, i], xin.at[k, i], x_send.at[k, i], x_recv.at[k, i], across[i])
        for cc in range(2):
            xs[k, cc] = summed(x, cc)

    def stage_y(k):
        yy = hi_of[k] * 2 + c
        for i in range(3):
            x_copies[k, i].wait_recv()
        for cc in range(2):
            ycode[k, cc] = encode(
                xs[k, cc] + decode(xin[k, 1, cc]) + decode(xin[k, 2, cc]) + decode(xin[k, 0, cc])
            )

            def start():
                remote(ycode.at[k, cc], yin.at[y], y_send.at[k, cc], y_recv.at[y], dev(yy, x, cc)).start()

            if k == 3:
                own = jnp.logical_and(c == ylo, c == cc)

                @pl.when(own)
                def _():
                    yin[y] = ycode[k, cc]

                pl.when(jnp.logical_not(own))(start)
            else:
                start()

    stage_sum(0)
    stage_sum(1)
    stage_sum(2)
    stage_sum(3)
    stage_y(0)
    stage_y(1)
    stage_y(2)
    stage_y(3)

    for cp in state_copies:
        cp.wait()
    t = step_ref[0]
    p1 = jnp.float32(1.0)
    p2 = jnp.float32(1.0)
    b1, b2 = 0.9, 0.95
    for bit in range(8):
        on = lax.rem(lax.shift_right_logical(t, bit), 2) == 1
        p1 = p1 * jnp.where(on, jnp.float32(b1), jnp.float32(1.0))
        p2 = p2 * jnp.where(on, jnp.float32(b2), jnp.float32(1.0))
        b1, b2 = b1 * b1, b2 * b2
    first_fix = jnp.full((J, 128), 1.0 - p1, F32)
    second_fix = jnp.full((J, 128), 1.0 - p2, F32)

    def y_wait(slot):
        remote(ycode.at[0, 0], yin.at[slot], y_send.at[0, 0], y_recv.at[slot], sibling).wait_recv()

    @pl.when(c != ylo)
    def _():
        y_wait(y)

    for d in FAR[::-1]:
        y_wait(lax.rem(y + d, 8))
    total = decode(yin[0])
    for i in range(1, 8):
        total = total + decode(yin[i])

    master = state[0]
    new_moment = 0.9 * state[1] + 0.1 * total
    new_second = 0.95 * state[2] + 0.05 * total * total
    update = new_moment / first_fix / (jnp.sqrt(new_second / second_fix) + 1e-08) + 0.1 * master
    new_master = master - 0.03 * update

    def row_of(yy, xx, cc):
        return lax.rem(yy, 2) * 32 + (yy // 2) * 8 + xx * 2 + cc

    me = row_of(y, x, c)
    rows[me] = new_master.astype(BF16)

    def pass_on(r, sem, where):
        send(rows.at[r], rows.at[r], sem, a_recv.at[r], where)

    def arrive(r):
        remote(rows.at[r], rows.at[r], ad_send.at[0], a_recv.at[r], sibling).wait_recv()

    for i, d in enumerate(FAR):
        pass_on(me, ay_send.at[i], dev(lax.rem(y + d, 8), x, c))

    def spread(i):
        r = row_of(lax.rem(y + ((0,) + FAR)[i], 8), x, c)
        if i:
            arrive(r)
        for q in range(3):
            pass_on(r, ax_send.at[q, i], across[q])
        pass_on(r, ad_send.at[i], sibling)

    def collect(i):
        yy = lax.rem(y + ((0,) + FAR)[i], 8)
        for q, xx in enumerate((xp, xm, xo)):
            r = row_of(yy, xx, c)
            arrive(r)
            pass_on(r, ad_send.at[8 + 3 * i + q], sibling)

    for i in range(8):
        spread(i)
    new_master_ref[...] = new_master
    new_moment_ref[...] = new_moment
    new_second_ref[...] = new_second
    for i in range(8):
        collect(i)
    for yy in range(8):
        for xx in range(4):
            arrive(row_of(yy, xx, oc))

    for cp in pending:
        cp.wait_send()
    for k in range(4):
        for cc in range(2):
            def done():
                remote(ycode.at[k, cc], yin.at[0], y_send.at[k, cc], y_recv.at[0], sibling).wait_send()

            if k == 3:
                pl.when(jnp.logical_not(jnp.logical_and(c == ylo, c == cc)))(done)
            else:
                done()


def write_out(
    m_ref, v_ref, s_ref, rows, m_out, v_out, s_out, p_out, wide, tiles, sems, tile_sems,
):
    small = [
        pltpu.make_async_copy(src, dst, sems.at[i])
        for i, (src, dst) in enumerate(((m_ref, m_out), (v_ref, v_out), (s_ref, s_out)))
    ]
    for cp in small:
        cp.start()
    copies = []
    for gp in range(4):
        for s in range(16):
            wide[gp % 2, s] = rows[gp * 16 + s].astype(F32)
        w = wide.at[gp % 2].reshape(16 * J, 128)
        for j in range(J):
            tiles[gp, :, pl.ds(j * 128, 128)] = w[pl.ds(j, 16, stride=J), :].astype(BF16)
        cp = pltpu.make_async_copy(tiles.at[gp], p_out.at[pl.ds(gp * 16, 16), :], tile_sems.at[gp])
        cp.start()
        copies.append(cp)
    for cp in small + copies:
        cp.wait()


def per_device(grads, master, moment, second, step):
    g = grads.reshape(8, 8, J, 128).transpose(0, 2, 1, 3)
    row = jax.ShapeDtypeStruct((J, 128), F32)
    vmem = pl.BlockSpec(memory_space=pltpu.VMEM)
    hbm = pl.BlockSpec(memory_space=pltpu.HBM)
    dma = pltpu.SemaphoreType.DMA
    parts = pl.pallas_call(
        reduce_update_gather,
        out_shape=(row, row, row, jax.ShapeDtypeStruct((64, J, 128), BF16)),
        in_specs=[hbm] * 5,
        out_specs=(vmem,) * 4,
        scratch_shapes=[
            pltpu.VMEM((4, J, 8, 128), F32),
            pltpu.VMEM((4, J, 8, 128), F32),
            pltpu.VMEM((4, 2, J, 128), F32),
            pltpu.VMEM((4, 3, 2, CODE, 128), I16),
            pltpu.VMEM((4, 3, 2, CODE, 128), I16),
            pltpu.VMEM((4, 2, CODE, 128), I16),
            pltpu.VMEM((8, CODE, 128), I16),
            pltpu.VMEM((3, J, 128), F32),
            pltpu.SMEM((1,), jnp.int32),
            dma((4,)), dma((4,)), dma((4,)), dma((4,)),
            dma((4, 3)), dma((4, 3)),
            dma((4, 2)), dma((8,)),
            dma((7,)), dma((64,)), dma((3, 8)), dma((32,)),
        ],
        compiler_params=pltpu.CompilerParams(
            collective_id=0, has_side_effects=True, vmem_limit_bytes=54500000
        ),
    )(step, g, master.reshape(J, 128), moment.reshape(J, 128), second.reshape(J, 128))
    new_master, new_moment, new_second, params = pl.pallas_call(
        write_out,
        out_shape=(row, row, row, jax.ShapeDtypeStruct((64, J * 128), BF16)),
        in_specs=[vmem] * 4,
        out_specs=(hbm,) * 4,
        scratch_shapes=[
            pltpu.VMEM((2, 16, J, 128), F32),
            pltpu.VMEM((4, 16, J * 128), BF16),
            dma((3,)), dma((4,)),
        ],
        compiler_params=pltpu.CompilerParams(vmem_limit_bytes=24 << 20),
    )(*parts)
    flat = (1, J * 128)
    return (new_master.reshape(flat), new_moment.reshape(flat), new_second.reshape(flat), params)


def solution(mesh):
    placed = (
        P(("section", "pair"), "dp", None, None),
        P(("section", "pair", "dp"), None),
        P(("section", "pair", "dp"), None),
        P(("section", "pair", "dp"), None),
        P("section"),
    )
    return jax.shard_map(
        per_device,
        mesh=mesh,
        in_specs=placed,
        out_specs=(
            P(("section", "pair", "dp"), None),
            P(("section", "pair", "dp"), None),
            P(("section", "pair", "dp"), None),
            P("section", None),
        ),
        check_vma=False,
    )
```

```python
import jax
import jax.numpy as jnp
from jax import lax
from jax.experimental import pallas as pl
from jax.experimental.pallas import tpu as pltpu
from jax.sharding import PartitionSpec as P

MESH = pl.DeviceIdType.MESH
F32 = jnp.float32
BF16 = jnp.bfloat16
I16 = jnp.int16
J = 56
CODE = 64
TOP = 32700.0
STEPS = 256.0
FAR = (1, 7, 2, 6, 3, 5, 4)
Y_ORDER = (4, 3, 5, 1, 7, 2, 6)
A_ORDER = ("c1", "c7", "o", "c2", "c6", "c3", "c5", "c4", "b", "g1", "g7", "g2", "g6", "k", "g3", "g5", "g4")


def encode(v):
    v = v.reshape(7, 8, 128)
    largest = jnp.maximum(jnp.max(jnp.abs(v), axis=0), 1e-30)
    e = jnp.ceil(jnp.log2(largest) * STEPS)
    q = jnp.round(v * (TOP * jnp.exp2(e * (-1.0 / STEPS)))[None])
    return jnp.concatenate([q.reshape(J, 128), e], axis=0).astype(jnp.int32).astype(I16)


def decode(code):
    f = code.astype(jnp.int32).astype(F32)
    scale = jnp.exp2(f[J:] * (1.0 / STEPS)) * (1.0 / TOP)
    return (f[:J].reshape(7, 8, 128) * scale[None]).reshape(J, 128)


def reduce_update_gather(
    step_ref, g_ref, master_hbm, moment_hbm, second_hbm,
    new_master_ref, new_moment_ref, new_second_ref, rows,
    mine, sib, xs, xcode, xin, ycode, yin, state,
    load_sem, state_sem, sent, d_recv, x_recv, y_recv, a_recv,
):
    ylo = lax.axis_index("pair")
    dp = lax.axis_index("dp")
    c = lax.rem(dp, 2)
    x = lax.rem(dp // 2, 4)
    yhi = dp // 8
    y = yhi * 2 + ylo
    oc = 1 - c
    xp = lax.rem(x + 1, 4)
    xm = lax.rem(x + 3, 4)
    xo = lax.rem(x + 2, 4)

    def dev(yy, xx, cc):
        return {"pair": lax.rem(yy, 2), "dp": ((yy // 2) * 4 + xx) * 2 + cc}

    sibling = dev(y, x, oc)
    across = [dev(y, xx, c) for xx in (xo, xp, xm)]

    def remote(src, dst, ssem, rsem, where):
        return pltpu.make_async_remote_copy(
            src_ref=src, dst_ref=dst, send_sem=ssem, recv_sem=rsem,
            device_id=where, device_id_type=MESH,
        )

    def wait_for(ref, sem):
        pltpu.make_async_copy(ref, ref, sem).wait()

    barrier = pltpu.get_barrier_semaphore()
    for where in [sibling] + across:
        pl.semaphore_signal(barrier, inc=1, device_id=where, device_id_type=MESH)
    for d in FAR:
        yy = lax.rem(y + d, 8)
        for cc in range(2):
            pl.semaphore_signal(barrier, inc=1, device_id=dev(yy, x, cc), device_id_type=MESH)

    hi_of = [lax.rem(yhi + d, 4) for d in (2, 1, 3, 0)]
    for k in range(4):
        pltpu.make_async_copy(g_ref.at[c * 4 + hi_of[k]], mine.at[k], load_sem.at[k]).start()
    for i, src in enumerate((master_hbm, moment_hbm, second_hbm)):
        pltpu.make_async_copy(src, state.at[i], state_sem).start()

    pl.semaphore_wait(barrier, 18)

    for k in range(4):
        remote(g_ref.at[oc * 4 + hi_of[k]], sib.at[k], sent.at[0], d_recv.at[k], sibling).start()

    def stage_sum(k):
        wait_for(mine.at[k], load_sem.at[k])
        wait_for(sib.at[k], d_recv.at[k])
        a = mine.at[k].reshape(J * 8, 128)
        b = sib.at[k].reshape(J * 8, 128)

        def summed(xx, cc):
            pieces = []
            for jb in range(7):
                sl = pl.ds(jb * 64 + xx * 2 + cc, 8, stride=8)
                pieces.append(a[sl, :] + b[sl, :])
            return jnp.concatenate(pieces, axis=0)

        for i, xx in enumerate((xo, xp, xm)):
            for cc in range(2):
                xcode[k, i, cc] = encode(summed(xx, cc))
            remote(xcode.at[k, i], xin.at[k, i], sent.at[1], x_recv.at[k], across[i]).start()
        for cc in range(2):
            xs[k, cc] = summed(x, cc)

    def stage_y(k):
        yy = hi_of[k] * 2 + c
        wait_for(xin.at[k], x_recv.at[k])
        for cc in range(2):
            ycode[k, cc] = encode(
                xs[k, cc] + decode(xin[k, 1, cc]) + decode(xin[k, 2, cc]) + decode(xin[k, 0, cc])
            )

            def start():
                remote(ycode.at[k, cc], yin.at[y], sent.at[2], y_recv, dev(yy, x, cc)).start()

            if k == 3:
                own = jnp.logical_and(c == ylo, c == cc)

                @pl.when(own)
                def _():
                    yin[y] = ycode[k, cc]

                pl.when(jnp.logical_not(own))(start)
            else:
                start()

    stage_sum(0)
    stage_sum(1)
    stage_sum(2)
    stage_sum(3)

    wait_for(state, state_sem)
    t = step_ref[0]
    p1 = jnp.float32(1.0)
    p2 = jnp.float32(1.0)
    b1, b2 = 0.9, 0.95
    for bit in range(8):
        on = lax.rem(lax.shift_right_logical(t, bit), 2) == 1
        p1 = p1 * jnp.where(on, jnp.float32(b1), jnp.float32(1.0))
        p2 = p2 * jnp.where(on, jnp.float32(b2), jnp.float32(1.0))
        b1, b2 = b1 * b1, b2 * b2
    first_fix = jnp.full((J, 128), 1.0 - p1, F32)
    second_fix = jnp.full((J, 128), 1.0 - p2, F32)

    stage_y(0)
    stage_y(1)
    stage_y(2)
    stage_y(3)

    def seven_or_eight(sem):
        @pl.when(c == ylo)
        def _():
            wait_for(yin.at[pl.ds(0, 7)], sem)

        @pl.when(c != ylo)
        def _():
            wait_for(yin, sem)

    seven_or_eight(y_recv)
    total = decode(yin[0])
    for i in range(1, 8):
        total = total + decode(yin[i])

    master = state[0]
    new_moment = 0.9 * state[1] + 0.1 * total
    new_second = 0.95 * state[2] + 0.05 * total * total
    update = new_moment / first_fix / (jnp.sqrt(new_second / second_fix) + 1e-08) + 0.1 * master
    new_master = master - 0.03 * update

    def row_of(yy, xx, cc):
        return lax.rem(yy, 2) * 32 + (yy // 2) * 8 + xx * 2 + cc

    slot = {d: i for i, d in enumerate((1, 2, 3, 4, 5, 6, 7))}
    COLUMN, GROUP, OPPOSITE, BESIDE, CORNER, SIBLING = 0, 7, 14, 15, 16, 17
    NEAR = (1, 7, 2, 6)

    def at_y(d):
        return lax.rem(y + d, 8)

    def pass_on(r, index, where):
        remote(rows.at[r], rows.at[r], sent.at[3], a_recv.at[index], where).start()

    def arrived(n, index):
        wait_for(rows.at[pl.ds(0, n)], a_recv.at[index])

    me = row_of(y, x, c)
    rows[me] = new_master.astype(BF16)
    for d in Y_ORDER:
        pass_on(me, COLUMN + slot[8 - d], dev(at_y(d), x, c))
    pass_on(me, OPPOSITE, across[0])
    pass_on(me, BESIDE, across[1])
    pass_on(me, BESIDE, across[2])
    pass_on(me, SIBLING, sibling)

    def column(d):
        arrived(1, COLUMN + slot[d])
        r = row_of(at_y(d), x, c)
        if d not in NEAR:
            pass_on(r, GROUP + slot[d], across[0])
        pass_on(r, GROUP + slot[d], across[1])
        pass_on(r, GROUP + slot[d], across[2])
        pass_on(r, SIBLING, sibling)

    def opposite():
        arrived(1, OPPOSITE)
        r = row_of(y, xo, c)
        for d in NEAR:
            pass_on(r, CORNER, dev(at_y(d), x, c))
        pass_on(r, SIBLING, sibling)

    def group(d):
        arrived(2 if d in NEAR else 3, GROUP + slot[d])
        pass_on(row_of(at_y(d), xp, c), SIBLING, sibling)
        pass_on(row_of(at_y(d), xm, c), SIBLING, sibling)
        if d not in NEAR:
            pass_on(row_of(at_y(d), xo, c), SIBLING, sibling)

    def beside():
        arrived(2, BESIDE)
        pass_on(row_of(y, xp, c), SIBLING, sibling)
        pass_on(row_of(y, xm, c), SIBLING, sibling)

    def corner():
        arrived(4, CORNER)
        for d in NEAR:
            pass_on(row_of(at_y(d), xo, c), SIBLING, sibling)

    steps = {"o": opposite, "b": beside, "k": corner}
    for what in A_ORDER:
        if what in steps:
            steps[what]()
        elif what[0] == "c":
            column(int(what[1]))
        else:
            group(int(what[1]))
    new_master_ref[...] = new_master
    new_moment_ref[...] = new_moment
    new_second_ref[...] = new_second
    arrived(32, SIBLING)

    wait_for(sib, sent.at[0])
    wait_for(xcode, sent.at[1])
    seven_or_eight(sent.at[2])
    wait_for(rows.at[pl.ds(0, 63)], sent.at[3])


def write_out(
    m_ref, v_ref, s_ref, rows, m_out, v_out, s_out, p_out, wide, tiles, sems, tile_sems,
):
    small = [
        pltpu.make_async_copy(src, dst, sems.at[i])
        for i, (src, dst) in enumerate(((m_ref, m_out), (v_ref, v_out), (s_ref, s_out)))
    ]
    for cp in small:
        cp.start()
    copies = []
    for gp in range(4):
        for s in range(16):
            wide[gp % 2, s] = rows[gp * 16 + s].astype(F32)
        w = wide.at[gp % 2].reshape(16 * J, 128)
        for j in range(J):
            tiles[gp, :, pl.ds(j * 128, 128)] = w[pl.ds(j, 16, stride=J), :].astype(BF16)
        cp = pltpu.make_async_copy(tiles.at[gp], p_out.at[pl.ds(gp * 16, 16), :], tile_sems.at[gp])
        cp.start()
        copies.append(cp)
    for cp in small + copies:
        cp.wait()


def per_device(grads, master, moment, second, step):
    g = grads.reshape(8, 8, J, 128).transpose(0, 2, 1, 3)
    row = jax.ShapeDtypeStruct((J, 128), F32)
    vmem = pl.BlockSpec(memory_space=pltpu.VMEM)
    hbm = pl.BlockSpec(memory_space=pltpu.HBM)
    dma = pltpu.SemaphoreType.DMA
    parts = pl.pallas_call(
        reduce_update_gather,
        out_shape=(row, row, row, jax.ShapeDtypeStruct((64, J, 128), BF16)),
        in_specs=[pl.BlockSpec(memory_space=pltpu.SMEM)] + [hbm] * 4,
        out_specs=(vmem,) * 4,
        scratch_shapes=[
            pltpu.VMEM((4, J, 8, 128), F32),
            pltpu.VMEM((4, J, 8, 128), F32),
            pltpu.VMEM((4, 2, J, 128), F32),
            pltpu.VMEM((4, 3, 2, CODE, 128), I16),
            pltpu.VMEM((4, 3, 2, CODE, 128), I16),
            pltpu.VMEM((4, 2, CODE, 128), I16),
            pltpu.VMEM((8, CODE, 128), I16),
            pltpu.VMEM((3, J, 128), F32),
            dma((4,)), dma, dma((4,)), dma((4,)), dma((4,)), dma, dma((18,)),
        ],
        compiler_params=pltpu.CompilerParams(
            collective_id=0, has_side_effects=True, vmem_limit_bytes=24 << 20
        ),
    )(step, *[
        pltpu.with_memory_space_constraint(a, pltpu.HBM)
        for a in (g, master.reshape(J, 128), moment.reshape(J, 128), second.reshape(J, 128))
    ])
    new_master, new_moment, new_second, params = pl.pallas_call(
        write_out,
        out_shape=(row, row, row, jax.ShapeDtypeStruct((64, J * 128), BF16)),
        in_specs=[vmem] * 4,
        out_specs=(hbm,) * 4,
        scratch_shapes=[
            pltpu.VMEM((2, 16, J, 128), F32),
            pltpu.VMEM((4, 16, J * 128), BF16),
            dma((3,)), dma((4,)),
        ],
        compiler_params=pltpu.CompilerParams(vmem_limit_bytes=24 << 20),
    )(*parts)
    flat = (1, J * 128)
    return (new_master.reshape(flat), new_moment.reshape(flat), new_second.reshape(flat), params)


def solution(mesh):
    placed = (
        P(("section", "pair"), "dp", None, None),
        P(("section", "pair", "dp"), None),
        P(("section", "pair", "dp"), None),
        P(("section", "pair", "dp"), None),
        P("section"),
    )
    return jax.shard_map(
        per_device,
        mesh=mesh,
        in_specs=placed,
        out_specs=(
            P(("section", "pair", "dp"), None),
            P(("section", "pair", "dp"), None),
            P(("section", "pair", "dp"), None),
            P("section", None),
        ),
        check_vma=False,
    )
```

```python
import jax
import jax.numpy as jnp
from jax import lax
from jax.experimental import pallas as pl
from jax.experimental.pallas import tpu as pltpu
from jax.sharding import PartitionSpec as P

MESH = pl.DeviceIdType.MESH
F32 = jnp.float32
BF16 = jnp.bfloat16
I16 = jnp.int16
J = 56
CODE = 64
TOP = 32700.0
STEPS = 256.0
FAR = (1, 7, 2, 6, 3, 5, 4)
Y_ORDER = (4, 3, 5, 1, 7, 2, 6)
A_ORDER = ("c1", "c7", "o", "c2", "c6", "c3", "c5", "c4", "b", "g1", "g7", "g2", "g6", "k", "g3", "g5", "g4")


def encode(v):
    v = v.reshape(7, 8, 128)
    largest = jnp.maximum(jnp.max(jnp.abs(v), axis=0), 1e-30)
    e = jnp.ceil(jnp.log2(largest) * STEPS)
    q = jnp.round(v * (TOP * jnp.exp2(e * (-1.0 / STEPS)))[None])
    return jnp.concatenate([q.reshape(J, 128), e], axis=0).astype(jnp.int32).astype(I16)


def decode(code):
    f = code.astype(jnp.int32).astype(F32)
    scale = jnp.exp2(f[J:] * (1.0 / STEPS)) * (1.0 / TOP)
    return (f[:J].reshape(7, 8, 128) * scale[None]).reshape(J, 128)


def reduce_update_gather(
    step_ref, g_ref, master_hbm, moment_hbm, second_hbm,
    new_master_ref, new_moment_ref, new_second_ref, rows,
    mine, sib, xs, xcode, xin, ycode, yin, state,
    load_sem, state_sem, sent, d_recv, x_recv, y_recv, a_recv, ready, told,
):
    ylo = lax.axis_index("pair")
    dp = lax.axis_index("dp")
    c = lax.rem(dp, 2)
    x = lax.rem(dp // 2, 4)
    yhi = dp // 8
    y = yhi * 2 + ylo
    oc = 1 - c
    xp = lax.rem(x + 1, 4)
    xm = lax.rem(x + 3, 4)
    xo = lax.rem(x + 2, 4)

    def dev(yy, xx, cc):
        return {"pair": lax.rem(yy, 2), "dp": ((yy // 2) * 4 + xx) * 2 + cc}

    sibling = dev(y, x, oc)
    across = [dev(y, xx, c) for xx in (xo, xp, xm)]

    def remote(src, dst, ssem, rsem, where):
        return pltpu.make_async_remote_copy(
            src_ref=src, dst_ref=dst, send_sem=ssem, recv_sem=rsem,
            device_id=where, device_id_type=MESH,
        )

    def wait_for(ref, sem):
        pltpu.make_async_copy(ref, ref, sem).wait()

    column_of = [dev(lax.rem(y + d, 8), x, 1) for d in FAR]
    row_mates = [dev(y, xx, 1) for xx in (xo, xp, xm)]

    def signal(sem, where):
        pl.semaphore_signal(sem, inc=1, device_id=where, device_id_type=MESH)

    barrier = pltpu.get_barrier_semaphore()
    signal(barrier, sibling)

    @pl.when(c == 1)
    def _():
        for where in row_mates + column_of:
            signal(barrier, where)

    hi_of = [lax.rem(yhi + d, 4) for d in (2, 1, 3, 0)]
    for k in range(4):
        pltpu.make_async_copy(g_ref.at[c * 4 + hi_of[k]], mine.at[k], load_sem.at[k]).start()
    for i, src in enumerate((master_hbm, moment_hbm, second_hbm)):
        pltpu.make_async_copy(src, state.at[i], state_sem).start()

    @pl.when(c == 1)
    def _():
        pl.semaphore_wait(barrier, 11)

    @pl.when(c == 0)
    def _():
        pl.semaphore_wait(barrier, 1)

    for k in range(4):
        remote(g_ref.at[oc * 4 + hi_of[k]], sib.at[k], sent.at[0], d_recv.at[k], sibling).start()

    @pl.when(c == 1)
    def _():
        for where in row_mates:
            signal(ready.at[0], where)
        for where in column_of:
            signal(ready.at[1], where)

    def tell(axis):
        @pl.when(c == 1)
        def _():
            pl.semaphore_wait(ready.at[axis], (3, 7)[axis])
            signal(told.at[axis], sibling)

    def told_of(axis):
        @pl.when(c == 0)
        def _():
            pl.semaphore_wait(told.at[axis], 1)

    tell(0)

    def stage_sum(k):
        wait_for(mine.at[k], load_sem.at[k])
        wait_for(sib.at[k], d_recv.at[k])
        a = mine.at[k].reshape(J * 8, 128)
        b = sib.at[k].reshape(J * 8, 128)

        def summed(xx, cc):
            pieces = []
            for jb in range(7):
                sl = pl.ds(jb * 64 + xx * 2 + cc, 8, stride=8)
                pieces.append(a[sl, :] + b[sl, :])
            return jnp.concatenate(pieces, axis=0)

        for i, xx in enumerate((xo, xp, xm)):
            for cc in range(2):
                xcode[k, i, cc] = encode(summed(xx, cc))
            if k == 0 and i == 0:
                told_of(0)
            remote(xcode.at[k, i], xin.at[k, i], sent.at[1], x_recv.at[k], across[i]).start()
        for cc in range(2):
            xs[k, cc] = summed(x, cc)

    def stage_y(k):
        yy = hi_of[k] * 2 + c
        wait_for(xin.at[k], x_recv.at[k])
        for cc in range(2):
            ycode[k, cc] = encode(
                xs[k, cc] + decode(xin[k, 1, cc]) + decode(xin[k, 2, cc]) + decode(xin[k, 0, cc])
            )

            def start():
                remote(ycode.at[k, cc], yin.at[y], sent.at[2], y_recv, dev(yy, x, cc)).start()

            if k == 3:
                own = jnp.logical_and(c == ylo, c == cc)

                @pl.when(own)
                def _():
                    yin[y] = ycode[k, cc]

                pl.when(jnp.logical_not(own))(start)
            else:
                start()

    stage_sum(0)
    stage_sum(1)
    stage_sum(2)
    stage_sum(3)

    tell(1)

    wait_for(state, state_sem)
    t = step_ref[0]
    p1 = jnp.float32(1.0)
    p2 = jnp.float32(1.0)
    b1, b2 = 0.9, 0.95
    for bit in range(8):
        on = lax.rem(lax.shift_right_logical(t, bit), 2) == 1
        p1 = p1 * jnp.where(on, jnp.float32(b1), jnp.float32(1.0))
        p2 = p2 * jnp.where(on, jnp.float32(b2), jnp.float32(1.0))
        b1, b2 = b1 * b1, b2 * b2
    first_fix = jnp.full((J, 128), 1.0 - p1, F32)
    second_fix = jnp.full((J, 128), 1.0 - p2, F32)

    told_of(1)
    stage_y(0)
    stage_y(1)
    stage_y(2)
    stage_y(3)

    def seven_or_eight(sem):
        @pl.when(c == ylo)
        def _():
            wait_for(yin.at[pl.ds(0, 7)], sem)

        @pl.when(c != ylo)
        def _():
            wait_for(yin, sem)

    seven_or_eight(y_recv)
    total = decode(yin[0])
    for i in range(1, 8):
        total = total + decode(yin[i])

    master = state[0]
    new_moment = 0.9 * state[1] + 0.1 * total
    new_second = 0.95 * state[2] + 0.05 * total * total
    update = new_moment / first_fix / (jnp.sqrt(new_second / second_fix) + 1e-08) + 0.1 * master
    new_master = master - 0.03 * update

    def row_of(yy, xx, cc):
        return lax.rem(yy, 2) * 32 + (yy // 2) * 8 + xx * 2 + cc

    slot = {d: i for i, d in enumerate((1, 2, 3, 4, 5, 6, 7))}
    COLUMN, GROUP, OPPOSITE, BESIDE, CORNER, SIBLING = 0, 7, 14, 15, 16, 17
    NEAR = (1, 7, 2, 6)

    def at_y(d):
        return lax.rem(y + d, 8)

    def pass_on(r, index, where):
        remote(rows.at[r], rows.at[r], sent.at[3], a_recv.at[index], where).start()

    def arrived(n, index):
        wait_for(rows.at[pl.ds(0, n)], a_recv.at[index])

    me = row_of(y, x, c)
    rows[me] = new_master.astype(BF16)
    for d in Y_ORDER:
        pass_on(me, COLUMN + slot[8 - d], dev(at_y(d), x, c))
    pass_on(me, OPPOSITE, across[0])
    pass_on(me, BESIDE, across[1])
    pass_on(me, BESIDE, across[2])
    pass_on(me, SIBLING, sibling)

    def column(d):
        arrived(1, COLUMN + slot[d])
        r = row_of(at_y(d), x, c)
        if d not in NEAR:
            pass_on(r, GROUP + slot[d], across[0])
        pass_on(r, GROUP + slot[d], across[1])
        pass_on(r, GROUP + slot[d], across[2])
        pass_on(r, SIBLING, sibling)

    def opposite():
        arrived(1, OPPOSITE)
        r = row_of(y, xo, c)
        for d in NEAR:
            pass_on(r, CORNER, dev(at_y(d), x, c))
        pass_on(r, SIBLING, sibling)

    def group(d):
        arrived(2 if d in NEAR else 3, GROUP + slot[d])
        pass_on(row_of(at_y(d), xp, c), SIBLING, sibling)
        pass_on(row_of(at_y(d), xm, c), SIBLING, sibling)
        if d not in NEAR:
            pass_on(row_of(at_y(d), xo, c), SIBLING, sibling)

    def beside():
        arrived(2, BESIDE)
        pass_on(row_of(y, xp, c), SIBLING, sibling)
        pass_on(row_of(y, xm, c), SIBLING, sibling)

    def corner():
        arrived(4, CORNER)
        for d in NEAR:
            pass_on(row_of(at_y(d), xo, c), SIBLING, sibling)

    steps = {"o": opposite, "b": beside, "k": corner}
    for what in A_ORDER:
        if what in steps:
            steps[what]()
        elif what[0] == "c":
            column(int(what[1]))
        else:
            group(int(what[1]))
    new_master_ref[...] = new_master
    new_moment_ref[...] = new_moment
    new_second_ref[...] = new_second
    arrived(32, SIBLING)

    wait_for(sib, sent.at[0])
    wait_for(xcode, sent.at[1])
    seven_or_eight(sent.at[2])
    wait_for(rows.at[pl.ds(0, 63)], sent.at[3])


def write_out(
    m_ref, v_ref, s_ref, rows, m_out, v_out, s_out, p_out, wide, tiles, sems, tile_sems,
):
    small = [
        pltpu.make_async_copy(src, dst, sems.at[i])
        for i, (src, dst) in enumerate(((m_ref, m_out), (v_ref, v_out), (s_ref, s_out)))
    ]
    for cp in small:
        cp.start()
    copies = []
    for gp in range(4):
        for s in range(16):
            wide[gp % 2, s] = rows[gp * 16 + s].astype(F32)
        w = wide.at[gp % 2].reshape(16 * J, 128)
        for j in range(J):
            tiles[gp, :, pl.ds(j * 128, 128)] = w[pl.ds(j, 16, stride=J), :].astype(BF16)
        cp = pltpu.make_async_copy(tiles.at[gp], p_out.at[pl.ds(gp * 16, 16), :], tile_sems.at[gp])
        cp.start()
        copies.append(cp)
    for cp in small + copies:
        cp.wait()


def per_device(grads, master, moment, second, step):
    g = grads.reshape(8, 8, J, 128).transpose(0, 2, 1, 3)
    row = jax.ShapeDtypeStruct((J, 128), F32)
    vmem = pl.BlockSpec(memory_space=pltpu.VMEM)
    hbm = pl.BlockSpec(memory_space=pltpu.HBM)
    dma = pltpu.SemaphoreType.DMA
    parts = pl.pallas_call(
        reduce_update_gather,
        out_shape=(row, row, row, jax.ShapeDtypeStruct((64, J, 128), BF16)),
        in_specs=[pl.BlockSpec(memory_space=pltpu.SMEM)] + [hbm] * 4,
        out_specs=(vmem,) * 4,
        scratch_shapes=[
            pltpu.VMEM((4, J, 8, 128), F32),
            pltpu.VMEM((4, J, 8, 128), F32),
            pltpu.VMEM((4, 2, J, 128), F32),
            pltpu.VMEM((4, 3, 2, CODE, 128), I16),
            pltpu.VMEM((4, 3, 2, CODE, 128), I16),
            pltpu.VMEM((4, 2, CODE, 128), I16),
            pltpu.VMEM((8, CODE, 128), I16),
            pltpu.VMEM((3, J, 128), F32),
            dma((4,)), dma, dma((4,)), dma((4,)), dma((4,)), dma, dma((18,)),
            pltpu.SemaphoreType.REGULAR((2,)), pltpu.SemaphoreType.REGULAR((2,)),
        ],
        compiler_params=pltpu.CompilerParams(
            collective_id=0, has_side_effects=True, vmem_limit_bytes=24 << 20
        ),
    )(step, *[
        pltpu.with_memory_space_constraint(a, pltpu.HBM)
        for a in (g, master.reshape(J, 128), moment.reshape(J, 128), second.reshape(J, 128))
    ])
    new_master, new_moment, new_second, params = pl.pallas_call(
        write_out,
        out_shape=(row, row, row, jax.ShapeDtypeStruct((64, J * 128), BF16)),
        in_specs=[vmem] * 4,
        out_specs=(hbm,) * 4,
        scratch_shapes=[
            pltpu.VMEM((2, 16, J, 128), F32),
            pltpu.VMEM((4, 16, J * 128), BF16),
            dma((3,)), dma((4,)),
        ],
        compiler_params=pltpu.CompilerParams(vmem_limit_bytes=24 << 20),
    )(*parts)
    flat = (1, J * 128)
    return (new_master.reshape(flat), new_moment.reshape(flat), new_second.reshape(flat), params)


def solution(mesh):
    placed = (
        P(("section", "pair"), "dp", None, None),
        P(("section", "pair", "dp"), None),
        P(("section", "pair", "dp"), None),
        P(("section", "pair", "dp"), None),
        P("section"),
    )
    return jax.shard_map(
        per_device,
        mesh=mesh,
        in_specs=placed,
        out_specs=(
            P(("section", "pair", "dp"), None),
            P(("section", "pair", "dp"), None),
            P(("section", "pair", "dp"), None),
            P("section", None),
        ),
        check_vma=False,
    )
```

```python
import jax
import jax.numpy as jnp
from jax import lax
from jax.experimental import pallas as pl
from jax.experimental.pallas import tpu as pltpu
from jax.sharding import PartitionSpec as P

MESH = pl.DeviceIdType.MESH
F32 = jnp.float32
BF16 = jnp.bfloat16
I16 = jnp.int16
J = 56
CODE = 64
TOP = 32700.0
STEPS = 256.0
FAR = (1, 7, 2, 6, 3, 5, 4)
Y_ORDER = (4, 3, 5, 1, 7, 2, 6)
A_ORDER = ("c1", "c7", "o", "c2", "c6", "c3", "c5", "c4", "b", "g1", "g7", "g2", "g6", "k", "g3", "g5", "g4")


def encode(v):
    v = v.reshape(7, 8, 128)
    largest = jnp.maximum(jnp.max(jnp.abs(v), axis=0), 1e-30)
    e = jnp.ceil(jnp.log2(largest) * STEPS)
    q = jnp.round(v * (TOP * jnp.exp2(e * (-1.0 / STEPS)))[None])
    return jnp.concatenate([q.reshape(J, 128), e], axis=0).astype(jnp.int32).astype(I16)


def decode(code):
    f = code.astype(jnp.int32).astype(F32)
    scale = jnp.exp2(f[J:] * (1.0 / STEPS)) * (1.0 / TOP)
    return (f[:J].reshape(7, 8, 128) * scale[None]).reshape(J, 128)


def reduce_update_gather(
    step_ref, g_ref, master_hbm, moment_hbm, second_hbm,
    new_master_ref, new_moment_ref, new_second_ref, rows,
    mine, sib, xs, xcode, xin, ycode, yin, state,
    load_sem, state_sem, sent, d_recv, x_recv, y_recv, a_recv, ready, told,
):
    ylo = lax.axis_index("pair")
    dp = lax.axis_index("dp")
    c = lax.rem(dp, 2)
    x = lax.rem(dp // 2, 4)
    yhi = dp // 8
    y = yhi * 2 + ylo
    oc = 1 - c
    xp = lax.rem(x + 1, 4)
    xm = lax.rem(x + 3, 4)
    xo = lax.rem(x + 2, 4)

    def dev(yy, xx, cc):
        return {"pair": lax.rem(yy, 2), "dp": ((yy // 2) * 4 + xx) * 2 + cc}

    sibling = dev(y, x, oc)
    across = [dev(y, xx, c) for xx in (xo, xp, xm)]

    def remote(src, dst, ssem, rsem, where):
        return pltpu.make_async_remote_copy(
            src_ref=src, dst_ref=dst, send_sem=ssem, recv_sem=rsem,
            device_id=where, device_id_type=MESH,
        )

    def wait_for(ref, sem):
        pltpu.make_async_copy(ref, ref, sem).wait()

    column_of = [dev(lax.rem(y + d, 8), x, 1) for d in FAR]
    row_mates = [dev(y, xx, 1) for xx in (xo, xp, xm)]

    def signal(sem, where):
        pl.semaphore_signal(sem, inc=1, device_id=where, device_id_type=MESH)

    barrier = pltpu.get_barrier_semaphore()
    signal(barrier, sibling)

    @pl.when(c == 1)
    def _():
        for where in row_mates + column_of:
            signal(barrier, where)

    hi_of = [lax.rem(yhi + d, 4) for d in (2, 3, 1, 0)]
    for k in range(4):
        pltpu.make_async_copy(g_ref.at[c * 4 + hi_of[k]], mine.at[k], load_sem.at[k]).start()
    for i, src in enumerate((master_hbm, moment_hbm, second_hbm)):
        pltpu.make_async_copy(src, state.at[i], state_sem).start()

    @pl.when(c == 1)
    def _():
        pl.semaphore_wait(barrier, 11)

    @pl.when(c == 0)
    def _():
        pl.semaphore_wait(barrier, 1)

    for k in range(4):
        remote(g_ref.at[oc * 4 + hi_of[k]], sib.at[k], sent.at[0], d_recv.at[k], sibling).start()

    @pl.when(c == 1)
    def _():
        for where, index in zip(row_mates, (0, 2, 1)):
            signal(ready.at[index], where)
        for where in column_of:
            signal(ready.at[3], where)

    def tell(index, count):
        pl.semaphore_wait(ready.at[index], count)
        signal(told.at[index], sibling)

    for i, xx in enumerate((xo, xp, xm)):
        @pl.when(jnp.logical_and(c == 1, xx != 0))
        def _(i=i):
            tell(i, 1)

    def send_x(k, i):
        remote(xcode.at[k, i], xin.at[k, i], sent.at[1], x_recv.at[k], across[i]).start()

    def stage_sum(k):
        wait_for(mine.at[k], load_sem.at[k])
        wait_for(sib.at[k], d_recv.at[k])
        a = mine.at[k].reshape(J * 8, 128)
        b = sib.at[k].reshape(J * 8, 128)

        def summed(xx, cc):
            pieces = []
            for jb in range(7):
                sl = pl.ds(jb * 64 + xx * 2 + cc, 8, stride=8)
                pieces.append(a[sl, :] + b[sl, :])
            return jnp.concatenate(pieces, axis=0)

        for i, xx in enumerate((xo, xp, xm)):
            for cc in range(2):
                xcode[k, i, cc] = encode(summed(xx, cc))

            @pl.when(xx != 0)
            def _(i=i):
                if k == 0:
                    @pl.when(c == 0)
                    def _():
                        pl.semaphore_wait(told.at[i], 1)
                send_x(k, i)
        for cc in range(2):
            xs[k, cc] = summed(x, cc)

    def stage_y(k):
        yy = hi_of[k] * 2 + c
        wait_for(xin.at[k], x_recv.at[k])
        for cc in range(2):
            ycode[k, cc] = encode(
                xs[k, cc] + decode(xin[k, 1, cc]) + decode(xin[k, 2, cc]) + decode(xin[k, 0, cc])
            )

            def start():
                remote(ycode.at[k, cc], yin.at[y], sent.at[2], y_recv, dev(yy, x, cc)).start()

            if k == 3:
                own = jnp.logical_and(c == ylo, c == cc)

                @pl.when(own)
                def _():
                    yin[y] = ycode[k, cc]

                pl.when(jnp.logical_not(own))(start)
            else:
                start()

    stage_sum(0)
    stage_sum(1)
    stage_sum(2)
    stage_sum(3)

    for i, xx in enumerate((xo, xp, xm)):
        @pl.when(xx == 0)
        def _(i=i):
            @pl.when(c == 1)
            def _():
                tell(i, 1)

            @pl.when(c == 0)
            def _():
                pl.semaphore_wait(told.at[i], 1)

            for k in range(4):
                send_x(k, i)

    @pl.when(c == 1)
    def _():
        tell(3, 7)

    wait_for(state, state_sem)
    t = step_ref[0]
    p1 = jnp.float32(1.0)
    p2 = jnp.float32(1.0)
    b1, b2 = 0.9, 0.95
    for bit in range(8):
        on = lax.rem(lax.shift_right_logical(t, bit), 2) == 1
        p1 = p1 * jnp.where(on, jnp.float32(b1), jnp.float32(1.0))
        p2 = p2 * jnp.where(on, jnp.float32(b2), jnp.float32(1.0))
        b1, b2 = b1 * b1, b2 * b2
    first_fix = jnp.full((J, 128), 1.0 - p1, F32)
    second_fix = jnp.full((J, 128), 1.0 - p2, F32)

    @pl.when(c == 0)
    def _():
        pl.semaphore_wait(told.at[3], 1)

    stage_y(0)
    stage_y(1)
    stage_y(2)
    stage_y(3)

    def seven_or_eight(sem):
        @pl.when(c == ylo)
        def _():
            wait_for(yin.at[pl.ds(0, 7)], sem)

        @pl.when(c != ylo)
        def _():
            wait_for(yin, sem)

    seven_or_eight(y_recv)
    total = decode(yin[0])
    for i in range(1, 8):
        total = total + decode(yin[i])

    master = state[0]
    new_moment = 0.9 * state[1] + 0.1 * total
    new_second = 0.95 * state[2] + 0.05 * total * total
    update = new_moment / first_fix / (jnp.sqrt(new_second / second_fix) + 1e-08) + 0.1 * master
    new_master = master - 0.03 * update

    def row_of(yy, xx, cc):
        return lax.rem(yy, 2) * 32 + (yy // 2) * 8 + xx * 2 + cc

    slot = {d: i for i, d in enumerate((1, 2, 3, 4, 5, 6, 7))}
    COLUMN, GROUP, OPPOSITE, BESIDE, CORNER, SIBLING = 0, 7, 14, 15, 16, 17
    NEAR = (1, 7, 2, 6)

    def at_y(d):
        return lax.rem(y + d, 8)

    def pass_on(r, index, where):
        remote(rows.at[r], rows.at[r], sent.at[3], a_recv.at[index], where).start()

    def arrived(n, index):
        wait_for(rows.at[pl.ds(0, n)], a_recv.at[index])

    me = row_of(y, x, c)
    rows[me] = new_master.astype(BF16)
    for d in Y_ORDER:
        pass_on(me, COLUMN + slot[8 - d], dev(at_y(d), x, c))
    pass_on(me, OPPOSITE, across[0])
    pass_on(me, BESIDE, across[1])
    pass_on(me, BESIDE, across[2])
    pass_on(me, SIBLING, sibling)

    def column(d):
        arrived(1, COLUMN + slot[d])
        r = row_of(at_y(d), x, c)
        if d not in NEAR:
            pass_on(r, GROUP + slot[d], across[0])
        pass_on(r, GROUP + slot[d], across[1])
        pass_on(r, GROUP + slot[d], across[2])
        pass_on(r, SIBLING, sibling)

    def opposite():
        arrived(1, OPPOSITE)
        r = row_of(y, xo, c)
        for d in NEAR:
            pass_on(r, CORNER, dev(at_y(d), x, c))
        pass_on(r, SIBLING, sibling)

    def group(d):
        arrived(2 if d in NEAR else 3, GROUP + slot[d])
        pass_on(row_of(at_y(d), xp, c), SIBLING, sibling)
        pass_on(row_of(at_y(d), xm, c), SIBLING, sibling)
        if d not in NEAR:
            pass_on(row_of(at_y(d), xo, c), SIBLING, sibling)

    def beside():
        arrived(2, BESIDE)
        pass_on(row_of(y, xp, c), SIBLING, sibling)
        pass_on(row_of(y, xm, c), SIBLING, sibling)

    def corner():
        arrived(4, CORNER)
        for d in NEAR:
            pass_on(row_of(at_y(d), xo, c), SIBLING, sibling)

    steps = {"o": opposite, "b": beside, "k": corner}
    for what in A_ORDER:
        if what in steps:
            steps[what]()
        elif what[0] == "c":
            column(int(what[1]))
        else:
            group(int(what[1]))
    new_master_ref[...] = new_master
    new_moment_ref[...] = new_moment
    new_second_ref[...] = new_second
    arrived(32, SIBLING)

    wait_for(sib, sent.at[0])
    wait_for(xcode, sent.at[1])
    seven_or_eight(sent.at[2])
    wait_for(rows.at[pl.ds(0, 63)], sent.at[3])


def write_out(
    m_ref, v_ref, s_ref, rows, m_out, v_out, s_out, p_out, wide, tiles, sems, tile_sems,
):
    small = [
        pltpu.make_async_copy(src, dst, sems.at[i])
        for i, (src, dst) in enumerate(((m_ref, m_out), (v_ref, v_out), (s_ref, s_out)))
    ]
    for cp in small:
        cp.start()
    copies = []
    for gp in range(4):
        for s in range(16):
            wide[gp % 2, s] = rows[gp * 16 + s].astype(F32)
        w = wide.at[gp % 2].reshape(16 * J, 128)
        for j in range(J):
            tiles[gp, :, pl.ds(j * 128, 128)] = w[pl.ds(j, 16, stride=J), :].astype(BF16)
        cp = pltpu.make_async_copy(tiles.at[gp], p_out.at[pl.ds(gp * 16, 16), :], tile_sems.at[gp])
        cp.start()
        copies.append(cp)
    for cp in small + copies:
        cp.wait()


def per_device(grads, master, moment, second, step):
    g = grads.reshape(8, 8, J, 128).transpose(0, 2, 1, 3)
    row = jax.ShapeDtypeStruct((J, 128), F32)
    vmem = pl.BlockSpec(memory_space=pltpu.VMEM)
    hbm = pl.BlockSpec(memory_space=pltpu.HBM)
    dma = pltpu.SemaphoreType.DMA
    parts = pl.pallas_call(
        reduce_update_gather,
        out_shape=(row, row, row, jax.ShapeDtypeStruct((64, J, 128), BF16)),
        in_specs=[pl.BlockSpec(memory_space=pltpu.SMEM)] + [hbm] * 4,
        out_specs=(vmem,) * 4,
        scratch_shapes=[
            pltpu.VMEM((4, J, 8, 128), F32),
            pltpu.VMEM((4, J, 8, 128), F32),
            pltpu.VMEM((4, 2, J, 128), F32),
            pltpu.VMEM((4, 3, 2, CODE, 128), I16),
            pltpu.VMEM((4, 3, 2, CODE, 128), I16),
            pltpu.VMEM((4, 2, CODE, 128), I16),
            pltpu.VMEM((8, CODE, 128), I16),
            pltpu.VMEM((3, J, 128), F32),
            dma((4,)), dma, dma((4,)), dma((4,)), dma((4,)), dma, dma((18,)),
            pltpu.SemaphoreType.REGULAR((4,)), pltpu.SemaphoreType.REGULAR((4,)),
        ],
        compiler_params=pltpu.CompilerParams(
            collective_id=0, has_side_effects=True, vmem_limit_bytes=24 << 20
        ),
    )(step, *[
        pltpu.with_memory_space_constraint(a, pltpu.HBM)
        for a in (g, master.reshape(J, 128), moment.reshape(J, 128), second.reshape(J, 128))
    ])
    new_master, new_moment, new_second, params = pl.pallas_call(
        write_out,
        out_shape=(row, row, row, jax.ShapeDtypeStruct((64, J * 128), BF16)),
        in_specs=[vmem] * 4,
        out_specs=(hbm,) * 4,
        scratch_shapes=[
            pltpu.VMEM((2, 16, J, 128), F32),
            pltpu.VMEM((4, 16, J * 128), BF16),
            dma((3,)), dma((4,)),
        ],
        compiler_params=pltpu.CompilerParams(vmem_limit_bytes=24 << 20),
    )(*parts)
    flat = (1, J * 128)
    return (new_master.reshape(flat), new_moment.reshape(flat), new_second.reshape(flat), params)


def solution(mesh):
    placed = (
        P(("section", "pair"), "dp", None, None),
        P(("section", "pair", "dp"), None),
        P(("section", "pair", "dp"), None),
        P(("section", "pair", "dp"), None),
        P("section"),
    )
    return jax.shard_map(
        per_device,
        mesh=mesh,
        in_specs=placed,
        out_specs=(
            P(("section", "pair", "dp"), None),
            P(("section", "pair", "dp"), None),
            P(("section", "pair", "dp"), None),
            P("section", None),
        ),
        check_vma=False,
    )
```

```python
import jax
import jax.numpy as jnp
from jax import lax
from jax.experimental import pallas as pl
from jax.experimental.pallas import tpu as pltpu
from jax.sharding import PartitionSpec as P

MESH = pl.DeviceIdType.MESH
F32 = jnp.float32
BF16 = jnp.bfloat16
I16 = jnp.int16
J = 56
CODE = 64
TOP = 32700.0
STEPS = 256.0
FAR = (1, 7, 2, 6, 3, 5, 4)
Y_ORDER = (4, 3, 5, 1, 7, 2, 6)
A_ORDER = ("c1", "c7", "o", "c2", "c6", "c3", "c5", "c4", "b", "g1", "g7", "g2", "g6", "k", "g3", "g5", "g4")


def encode(v):
    v = v.reshape(7, 8, 128)
    largest = jnp.maximum(jnp.max(jnp.abs(v), axis=0), 1e-30)
    e = jnp.ceil(jnp.log2(largest) * STEPS)
    q = jnp.round(v * (TOP * jnp.exp2(e * (-1.0 / STEPS)))[None])
    return jnp.concatenate([q.reshape(J, 128), e], axis=0).astype(jnp.int32).astype(I16)


def decode(code):
    f = code.astype(jnp.int32).astype(F32)
    scale = jnp.exp2(f[J:] * (1.0 / STEPS)) * (1.0 / TOP)
    return (f[:J].reshape(7, 8, 128) * scale[None]).reshape(J, 128)


def reduce_update_gather(
    step_ref, g_ref, master_hbm, moment_hbm, second_hbm,
    new_master_ref, new_moment_ref, new_second_ref, rows,
    mine, sib, xs, xcode, xin, ycode, yin, din, part, state,
    load_sem, state_sem, sent, d_recv, x_recv, y_recv, din_recv, a_recv, ready, told,
):
    ylo = lax.axis_index("pair")
    dp = lax.axis_index("dp")
    c = lax.rem(dp, 2)
    x = lax.rem(dp // 2, 4)
    yhi = dp // 8
    y = yhi * 2 + ylo
    oc = 1 - c
    xp = lax.rem(x + 1, 4)
    xm = lax.rem(x + 3, 4)
    xo = lax.rem(x + 2, 4)

    def dev(yy, xx, cc):
        return {"pair": lax.rem(yy, 2), "dp": ((yy // 2) * 4 + xx) * 2 + cc}

    sibling = dev(y, x, oc)
    across = [dev(y, xx, c) for xx in (xo, xp, xm)]

    def remote(src, dst, ssem, rsem, where):
        return pltpu.make_async_remote_copy(
            src_ref=src, dst_ref=dst, send_sem=ssem, recv_sem=rsem,
            device_id=where, device_id_type=MESH,
        )

    def wait_for(ref, sem):
        pltpu.make_async_copy(ref, ref, sem).wait()

    both, either = jnp.logical_and, jnp.logical_or
    base = y == 0
    first = both(base, x == 0)
    mate = both(base, x != 0)
    above = both(x == 0, y != 0)
    direct = [both(base, either(x == 0, xx == 0)) for xx in (xo, xp, xm)]

    column_of = [dev(lax.rem(y + d, 8), x, 1) for d in FAR]
    row_mates = [dev(y, xx, 1) for xx in (xo, xp, xm)]

    def signal(sem, where):
        pl.semaphore_signal(sem, inc=1, device_id=where, device_id_type=MESH)

    barrier = pltpu.get_barrier_semaphore()
    signal(barrier, sibling)

    @pl.when(c == 1)
    def _():
        for where in row_mates + column_of:
            signal(barrier, where)

    hi_of = [lax.rem(yhi + d, 4) for d in (2, 3, 1, 0)]
    for k in range(4):
        pltpu.make_async_copy(g_ref.at[c * 4 + hi_of[k]], mine.at[k], load_sem.at[k]).start()
    for i, src in enumerate((master_hbm, moment_hbm, second_hbm)):
        pltpu.make_async_copy(src, state.at[i], state_sem).start()

    @pl.when(c == 1)
    def _():
        pl.semaphore_wait(barrier, 11)

    @pl.when(c == 0)
    def _():
        pl.semaphore_wait(barrier, 1)

    for k in range(4):
        remote(g_ref.at[oc * 4 + hi_of[k]], sib.at[k], sent.at[0], d_recv.at[k], sibling).start()

    @pl.when(c == 1)
    def _():
        for where in row_mates:
            signal(ready.at[first.astype(jnp.int32)], where)
        for where in column_of:
            signal(ready.at[2 - first.astype(jnp.int32)], where)

        @pl.when(mate)
        def _():
            pl.semaphore_wait(ready.at[0], 2)

        @pl.when(jnp.logical_not(mate))
        def _():
            pl.semaphore_wait(ready.at[0], 3)

        @pl.when(base)
        def _():
            pl.semaphore_wait(ready.at[3], 7)

        @pl.when(jnp.logical_not(base))
        def _():
            signal(ready.at[3], dev(0, x, 1))

        signal(told.at[0], sibling)

    def send_direct(k, i, xx):
        for cc in range(2):
            remote(
                xcode.at[k, i, cc], din.at[x], sent.at[1], din_recv, dev(hi_of[k] * 2 + c, xx, cc)
            ).start()

    def send_x(k, i):
        remote(xcode.at[k, i], xin.at[k, i], sent.at[1], x_recv.at[k], across[i]).start()

    def stage_sum(k):
        wait_for(mine.at[k], load_sem.at[k])
        wait_for(sib.at[k], d_recv.at[k])
        a = mine.at[k].reshape(J * 8, 128)
        b = sib.at[k].reshape(J * 8, 128)

        def summed(xx, cc):
            pieces = []
            for jb in range(7):
                sl = pl.ds(jb * 64 + xx * 2 + cc, 8, stride=8)
                pieces.append(a[sl, :] + b[sl, :])
            return jnp.concatenate(pieces, axis=0)

        for i, xx in enumerate((xo, xp, xm)):
            for cc in range(2):
                xcode[k, i, cc] = encode(summed(xx, cc))

            if k == 0 and i == 0:
                @pl.when(c == 0)
                def _():
                    pl.semaphore_wait(told.at[0], 1)

            now = direct[i]
            if k == 3:
                now = both(now, jnp.logical_not(both(xx == 0, hi_of[k] * 2 + c == 0)))

            @pl.when(now)
            def _(i=i, xx=xx):
                send_direct(k, i, xx)

            @pl.when(jnp.logical_not(direct[i]))
            def _(i=i):
                send_x(k, i)

        for cc in range(2):
            xs[k, cc] = summed(x, cc)

    def stage_y(k):
        yy = hi_of[k] * 2 + c
        @pl.when(jnp.logical_not(base))
        def _():
            wait_for(xin.at[k], x_recv.at[k])

        @pl.when(mate)
        def _():
            wait_for(xin.at[k, pl.ds(0, 2)], x_recv.at[k])

        for i, sender in enumerate((0, 2, 1)):
            @pl.when(jnp.logical_not(direct[sender]))
            def _(i=i):
                for cc in range(2):
                    xs[k, cc] = xs[k, cc] + decode(xin[k, i, cc])

        for cc in range(2):
            ycode[k, cc] = encode(xs[k, cc])

        if k == 3:
            for cc in range(2):
                own = both(c == ylo, c == cc)

                @pl.when(own)
                def _(cc=cc):
                    yin[y] = ycode[k, cc]

                @pl.when(jnp.logical_not(either(own, both(above, yy == 0))))
                def _(cc=cc):
                    send_y(k, cc)
        else:
            @pl.when(jnp.logical_not(both(above, yy == 0)))
            def _():
                for cc in range(2):
                    send_y(k, cc)

    def send_y(k, cc):
        remote(
            ycode.at[k, cc], yin.at[y], sent.at[2], y_recv, dev(hi_of[k] * 2 + c, x, cc)
        ).start()

    stage_sum(0)
    stage_sum(1)
    stage_sum(2)
    stage_sum(3)

    @pl.when(c == 1)
    def _():
        @pl.when(above)
        def _():
            pl.semaphore_wait(ready.at[2], 6)

        @pl.when(jnp.logical_not(above))
        def _():
            pl.semaphore_wait(ready.at[2], 7)

        signal(told.at[2], sibling)

    wait_for(state, state_sem)
    t = step_ref[0]
    p1 = jnp.float32(1.0)
    p2 = jnp.float32(1.0)
    b1, b2 = 0.9, 0.95
    for bit in range(8):
        on = lax.rem(lax.shift_right_logical(t, bit), 2) == 1
        p1 = p1 * jnp.where(on, jnp.float32(b1), jnp.float32(1.0))
        p2 = p2 * jnp.where(on, jnp.float32(b2), jnp.float32(1.0))
        b1, b2 = b1 * b1, b2 * b2
    first_fix = jnp.full((J, 128), 1.0 - p1, F32)
    second_fix = jnp.full((J, 128), 1.0 - p2, F32)

    @pl.when(c == 0)
    def _():
        pl.semaphore_wait(told.at[2], 1)

    stage_y(0)
    stage_y(1)
    stage_y(2)
    stage_y(3)

    @pl.when(either(mate, above))
    def _():
        @pl.when(c == 1)
        def _():
            pl.semaphore_wait(ready.at[1], 1)
            signal(told.at[1], sibling)

        @pl.when(c == 0)
        def _():
            pl.semaphore_wait(told.at[1], 1)
            for i, xx in enumerate((xo, xp, xm)):
                @pl.when(both(mate, xx == 0))
                def _(i=i, xx=xx):
                    send_direct(3, i, xx)

            for k in range(4):
                @pl.when(both(above, hi_of[k] == 0))
                def _(k=k):
                    for cc in range(2):
                        send_y(k, cc)

    def seven_or_eight(sem):
        @pl.when(c == ylo)
        def _():
            wait_for(yin.at[pl.ds(0, 7)], sem)

        @pl.when(c != ylo)
        def _():
            wait_for(yin, sem)

    @pl.when(x == 0)
    def _():
        wait_for(din.at[pl.ds(0, 3)], din_recv)
        part[...] = decode(din[1]) + decode(din[2]) + decode(din[3])

    seven_or_eight(y_recv)

    @pl.when(x != 0)
    def _():
        wait_for(din.at[0], din_recv)
        part[...] = decode(din[0])

    total = part[...]
    for i in range(8):
        total = total + decode(yin[i])

    master = state[0]
    new_moment = 0.9 * state[1] + 0.1 * total
    new_second = 0.95 * state[2] + 0.05 * total * total
    update = new_moment / first_fix / (jnp.sqrt(new_second / second_fix) + 1e-08) + 0.1 * master
    new_master = master - 0.03 * update

    def row_of(yy, xx, cc):
        return lax.rem(yy, 2) * 32 + (yy // 2) * 8 + xx * 2 + cc

    slot = {d: i for i, d in enumerate((1, 2, 3, 4, 5, 6, 7))}
    COLUMN, GROUP, OPPOSITE, BESIDE, CORNER, SIBLING = 0, 7, 14, 15, 16, 17
    NEAR = (1, 7, 2, 6)

    def at_y(d):
        return lax.rem(y + d, 8)

    def pass_on(r, index, where):
        remote(rows.at[r], rows.at[r], sent.at[3], a_recv.at[index], where).start()

    def arrived(n, index):
        wait_for(rows.at[pl.ds(0, n)], a_recv.at[index])

    me = row_of(y, x, c)
    rows[me] = new_master.astype(BF16)
    for d in Y_ORDER:
        pass_on(me, COLUMN + slot[8 - d], dev(at_y(d), x, c))
    pass_on(me, OPPOSITE, across[0])
    pass_on(me, BESIDE, across[1])
    pass_on(me, BESIDE, across[2])
    pass_on(me, SIBLING, sibling)

    def column(d):
        arrived(1, COLUMN + slot[d])
        r = row_of(at_y(d), x, c)
        if d not in NEAR:
            pass_on(r, GROUP + slot[d], across[0])
        pass_on(r, GROUP + slot[d], across[1])
        pass_on(r, GROUP + slot[d], across[2])
        pass_on(r, SIBLING, sibling)

    def opposite():
        arrived(1, OPPOSITE)
        r = row_of(y, xo, c)
        for d in NEAR:
            pass_on(r, CORNER, dev(at_y(d), x, c))
        pass_on(r, SIBLING, sibling)

    def group(d):
        arrived(2 if d in NEAR else 3, GROUP + slot[d])
        pass_on(row_of(at_y(d), xp, c), SIBLING, sibling)
        pass_on(row_of(at_y(d), xm, c), SIBLING, sibling)
        if d not in NEAR:
            pass_on(row_of(at_y(d), xo, c), SIBLING, sibling)

    def beside():
        arrived(2, BESIDE)
        pass_on(row_of(y, xp, c), SIBLING, sibling)
        pass_on(row_of(y, xm, c), SIBLING, sibling)

    def corner():
        arrived(4, CORNER)
        for d in NEAR:
            pass_on(row_of(at_y(d), xo, c), SIBLING, sibling)

    steps = {"o": opposite, "b": beside, "k": corner}
    for what in A_ORDER:
        if what in steps:
            steps[what]()
        elif what[0] == "c":
            column(int(what[1]))
        else:
            group(int(what[1]))
    new_master_ref[...] = new_master
    new_moment_ref[...] = new_moment
    new_second_ref[...] = new_second
    arrived(32, SIBLING)

    wait_for(sib, sent.at[0])
    wait_for(xcode, sent.at[1])
    seven_or_eight(sent.at[2])
    wait_for(rows.at[pl.ds(0, 63)], sent.at[3])


def write_out(
    m_ref, v_ref, s_ref, rows, m_out, v_out, s_out, p_out, wide, tiles, sems, tile_sems,
):
    small = [
        pltpu.make_async_copy(src, dst, sems.at[i])
        for i, (src, dst) in enumerate(((m_ref, m_out), (v_ref, v_out), (s_ref, s_out)))
    ]
    for cp in small:
        cp.start()
    copies = []
    for gp in range(4):
        for s in range(16):
            wide[gp % 2, s] = rows[gp * 16 + s].astype(F32)
        w = wide.at[gp % 2].reshape(16 * J, 128)
        for j in range(J):
            tiles[gp, :, pl.ds(j * 128, 128)] = w[pl.ds(j, 16, stride=J), :].astype(BF16)
        cp = pltpu.make_async_copy(tiles.at[gp], p_out.at[pl.ds(gp * 16, 16), :], tile_sems.at[gp])
        cp.start()
        copies.append(cp)
    for cp in small + copies:
        cp.wait()


def per_device(grads, master, moment, second, step):
    g = grads.reshape(8, 8, J, 128).transpose(0, 2, 1, 3)
    row = jax.ShapeDtypeStruct((J, 128), F32)
    vmem = pl.BlockSpec(memory_space=pltpu.VMEM)
    hbm = pl.BlockSpec(memory_space=pltpu.HBM)
    dma = pltpu.SemaphoreType.DMA
    parts = pl.pallas_call(
        reduce_update_gather,
        out_shape=(row, row, row, jax.ShapeDtypeStruct((64, J, 128), BF16)),
        in_specs=[pl.BlockSpec(memory_space=pltpu.SMEM)] + [hbm] * 4,
        out_specs=(vmem,) * 4,
        scratch_shapes=[
            pltpu.VMEM((4, J, 8, 128), F32),
            pltpu.VMEM((4, J, 8, 128), F32),
            pltpu.VMEM((4, 2, J, 128), F32),
            pltpu.VMEM((4, 3, 2, CODE, 128), I16),
            pltpu.VMEM((4, 3, 2, CODE, 128), I16),
            pltpu.VMEM((4, 2, CODE, 128), I16),
            pltpu.VMEM((8, CODE, 128), I16),
            pltpu.VMEM((4, CODE, 128), I16),
            pltpu.VMEM((J, 128), F32),
            pltpu.VMEM((3, J, 128), F32),
            dma((4,)), dma, dma((4,)), dma((4,)), dma((4,)), dma, dma, dma((18,)),
            pltpu.SemaphoreType.REGULAR((4,)), pltpu.SemaphoreType.REGULAR((4,)),
        ],
        compiler_params=pltpu.CompilerParams(
            collective_id=0, has_side_effects=True, vmem_limit_bytes=24 << 20
        ),
    )(step, *[
        pltpu.with_memory_space_constraint(a, pltpu.HBM)
        for a in (g, master.reshape(J, 128), moment.reshape(J, 128), second.reshape(J, 128))
    ])
    new_master, new_moment, new_second, params = pl.pallas_call(
        write_out,
        out_shape=(row, row, row, jax.ShapeDtypeStruct((64, J * 128), BF16)),
        in_specs=[vmem] * 4,
        out_specs=(hbm,) * 4,
        scratch_shapes=[
            pltpu.VMEM((2, 16, J, 128), F32),
            pltpu.VMEM((4, 16, J * 128), BF16),
            dma((3,)), dma((4,)),
        ],
        compiler_params=pltpu.CompilerParams(vmem_limit_bytes=24 << 20),
    )(*parts)
    flat = (1, J * 128)
    return (new_master.reshape(flat), new_moment.reshape(flat), new_second.reshape(flat), params)


def solution(mesh):
    placed = (
        P(("section", "pair"), "dp", None, None),
        P(("section", "pair", "dp"), None),
        P(("section", "pair", "dp"), None),
        P(("section", "pair", "dp"), None),
        P("section"),
    )
    return jax.shard_map(
        per_device,
        mesh=mesh,
        in_specs=placed,
        out_specs=(
            P(("section", "pair", "dp"), None),
            P(("section", "pair", "dp"), None),
            P(("section", "pair", "dp"), None),
            P("section", None),
        ),
        check_vma=False,
    )
```

```python
import jax
import jax.numpy as jnp
from jax import lax
from jax.experimental import pallas as pl
from jax.experimental.pallas import tpu as pltpu
from jax.sharding import PartitionSpec as P

MESH = pl.DeviceIdType.MESH
F32 = jnp.float32
BF16 = jnp.bfloat16
I16 = jnp.int16
J = 56
CODE = 64
TOP = 32700.0
STEPS = 256.0
FAR = (1, 7, 2, 6, 3, 5, 4)
Y_ORDER = (4, 3, 5, 1, 7, 2, 6)
A_ORDER = ("c1", "c7", "o", "c2", "c6", "c3", "c5", "c4", "b", "g1", "g7", "g2", "g6", "k", "g3", "g5", "g4")


def encode(v):
    v = v.reshape(7, 8, 128)
    largest = jnp.maximum(jnp.max(jnp.abs(v), axis=0), 1e-30)
    e = jnp.ceil(jnp.log2(largest) * STEPS)
    q = jnp.round(v * (TOP * jnp.exp2(e * (-1.0 / STEPS)))[None])
    return jnp.concatenate([q.reshape(J, 128), e], axis=0).astype(jnp.int32).astype(I16)


def decode(code):
    f = code.astype(jnp.int32).astype(F32)
    scale = jnp.exp2(f[J:] * (1.0 / STEPS)) * (1.0 / TOP)
    return (f[:J].reshape(7, 8, 128) * scale[None]).reshape(J, 128)


def reduce_update_gather(
    step_ref, g_ref, master_hbm, moment_hbm, second_hbm,
    new_master_ref, new_moment_ref, new_second_ref, tiles,
    rows, wide, mine, sib, xs, xcode, xin, ycode, yin, din, part, state,
    load_sem, state_sem, sent, d_recv, x_recv, y_recv, din_recv, a_recv, ready, told,
):
    ylo = lax.axis_index("pair")
    dp = lax.axis_index("dp")
    c = lax.rem(dp, 2)
    x = lax.rem(dp // 2, 4)
    yhi = dp // 8
    y = yhi * 2 + ylo
    oc = 1 - c
    xp = lax.rem(x + 1, 4)
    xm = lax.rem(x + 3, 4)
    xo = lax.rem(x + 2, 4)

    def dev(yy, xx, cc):
        return {"pair": lax.rem(yy, 2), "dp": ((yy // 2) * 4 + xx) * 2 + cc}

    sibling = dev(y, x, oc)
    across = [dev(y, xx, c) for xx in (xo, xp, xm)]

    def remote(src, dst, ssem, rsem, where):
        return pltpu.make_async_remote_copy(
            src_ref=src, dst_ref=dst, send_sem=ssem, recv_sem=rsem,
            device_id=where, device_id_type=MESH,
        )

    def wait_for(ref, sem):
        pltpu.make_async_copy(ref, ref, sem).wait()

    both, either = jnp.logical_and, jnp.logical_or
    base = y == 0
    first = both(base, x == 0)
    mate = both(base, x != 0)
    above = both(x == 0, y != 0)
    direct = [both(base, either(x == 0, xx == 0)) for xx in (xo, xp, xm)]

    column_of = [dev(lax.rem(y + d, 8), x, 1) for d in FAR]
    row_mates = [dev(y, xx, 1) for xx in (xo, xp, xm)]

    def signal(sem, where):
        pl.semaphore_signal(sem, inc=1, device_id=where, device_id_type=MESH)

    barrier = pltpu.get_barrier_semaphore()
    signal(barrier, sibling)

    @pl.when(c == 1)
    def _():
        for where in row_mates + column_of:
            signal(barrier, where)

    hi_of = [lax.rem(yhi + d, 4) for d in (2, 3, 1, 0)]
    for k in range(4):
        pltpu.make_async_copy(g_ref.at[c * 4 + hi_of[k]], mine.at[k], load_sem.at[k]).start()
    for i, src in enumerate((master_hbm, moment_hbm, second_hbm)):
        pltpu.make_async_copy(src, state.at[i], state_sem).start()

    @pl.when(c == 1)
    def _():
        pl.semaphore_wait(barrier, 11)

    @pl.when(c == 0)
    def _():
        pl.semaphore_wait(barrier, 1)

    for k in range(4):
        remote(g_ref.at[oc * 4 + hi_of[k]], sib.at[k], sent.at[0], d_recv.at[k], sibling).start()

    @pl.when(c == 1)
    def _():
        for where in row_mates:
            signal(ready.at[first.astype(jnp.int32)], where)
        for where in column_of:
            signal(ready.at[2 - first.astype(jnp.int32)], where)

        @pl.when(mate)
        def _():
            pl.semaphore_wait(ready.at[0], 2)

        @pl.when(jnp.logical_not(mate))
        def _():
            pl.semaphore_wait(ready.at[0], 3)

        @pl.when(base)
        def _():
            pl.semaphore_wait(ready.at[3], 7)

        @pl.when(jnp.logical_not(base))
        def _():
            signal(ready.at[3], dev(0, x, 1))

        signal(told.at[0], sibling)

    def send_direct(k, i, xx):
        for cc in range(2):
            remote(
                xcode.at[k, i, cc], din.at[x], sent.at[1], din_recv, dev(hi_of[k] * 2 + c, xx, cc)
            ).start()

    def send_x(k, i):
        remote(xcode.at[k, i], xin.at[k, i], sent.at[1], x_recv.at[k], across[i]).start()

    def stage_sum(k):
        wait_for(mine.at[k], load_sem.at[k])
        wait_for(sib.at[k], d_recv.at[k])
        a = mine.at[k].reshape(J * 8, 128)
        b = sib.at[k].reshape(J * 8, 128)

        def summed(xx, cc):
            pieces = []
            for jb in range(7):
                sl = pl.ds(jb * 64 + xx * 2 + cc, 8, stride=8)
                pieces.append(a[sl, :] + b[sl, :])
            return jnp.concatenate(pieces, axis=0)

        for i, xx in enumerate((xo, xp, xm)):
            for cc in range(2):
                xcode[k, i, cc] = encode(summed(xx, cc))

            if k == 0 and i == 0:
                @pl.when(c == 0)
                def _():
                    pl.semaphore_wait(told.at[0], 1)

            now = direct[i]
            if k == 3:
                now = both(now, jnp.logical_not(both(xx == 0, hi_of[k] * 2 + c == 0)))

            @pl.when(now)
            def _(i=i, xx=xx):
                send_direct(k, i, xx)

            @pl.when(jnp.logical_not(direct[i]))
            def _(i=i):
                send_x(k, i)

        for cc in range(2):
            xs[k, cc] = summed(x, cc)

    def stage_y(k):
        yy = hi_of[k] * 2 + c
        @pl.when(jnp.logical_not(base))
        def _():
            wait_for(xin.at[k], x_recv.at[k])

        @pl.when(mate)
        def _():
            wait_for(xin.at[k, pl.ds(0, 2)], x_recv.at[k])

        for i, sender in enumerate((0, 2, 1)):
            @pl.when(jnp.logical_not(direct[sender]))
            def _(i=i):
                for cc in range(2):
                    xs[k, cc] = xs[k, cc] + decode(xin[k, i, cc])

        for cc in range(2):
            ycode[k, cc] = encode(xs[k, cc])

        if k == 3:
            for cc in range(2):
                own = both(c == ylo, c == cc)

                @pl.when(own)
                def _(cc=cc):
                    yin[y] = ycode[k, cc]

                @pl.when(jnp.logical_not(either(own, both(above, yy == 0))))
                def _(cc=cc):
                    send_y(k, cc)
        else:
            @pl.when(jnp.logical_not(both(above, yy == 0)))
            def _():
                for cc in range(2):
                    send_y(k, cc)

    def send_y(k, cc):
        remote(
            ycode.at[k, cc], yin.at[y], sent.at[2], y_recv, dev(hi_of[k] * 2 + c, x, cc)
        ).start()

    stage_sum(0)
    stage_sum(1)
    stage_sum(2)
    stage_sum(3)

    @pl.when(c == 1)
    def _():
        @pl.when(above)
        def _():
            pl.semaphore_wait(ready.at[2], 6)

        @pl.when(jnp.logical_not(above))
        def _():
            pl.semaphore_wait(ready.at[2], 7)

        signal(told.at[2], sibling)

    wait_for(state, state_sem)
    t = step_ref[0]
    p1 = jnp.float32(1.0)
    p2 = jnp.float32(1.0)
    b1, b2 = 0.9, 0.95
    for bit in range(8):
        on = lax.rem(lax.shift_right_logical(t, bit), 2) == 1
        p1 = p1 * jnp.where(on, jnp.float32(b1), jnp.float32(1.0))
        p2 = p2 * jnp.where(on, jnp.float32(b2), jnp.float32(1.0))
        b1, b2 = b1 * b1, b2 * b2
    first_fix = jnp.full((J, 128), 1.0 - p1, F32)
    second_fix = jnp.full((J, 128), 1.0 - p2, F32)

    @pl.when(c == 0)
    def _():
        pl.semaphore_wait(told.at[2], 1)

    stage_y(0)
    stage_y(1)
    stage_y(2)
    stage_y(3)

    @pl.when(either(mate, above))
    def _():
        @pl.when(c == 1)
        def _():
            pl.semaphore_wait(ready.at[1], 1)
            signal(told.at[1], sibling)

        @pl.when(c == 0)
        def _():
            pl.semaphore_wait(told.at[1], 1)
            for i, xx in enumerate((xo, xp, xm)):
                @pl.when(both(mate, xx == 0))
                def _(i=i, xx=xx):
                    send_direct(3, i, xx)

            for k in range(4):
                @pl.when(both(above, hi_of[k] == 0))
                def _(k=k):
                    for cc in range(2):
                        send_y(k, cc)

    def seven_or_eight(sem):
        @pl.when(c == ylo)
        def _():
            wait_for(yin.at[pl.ds(0, 7)], sem)

        @pl.when(c != ylo)
        def _():
            wait_for(yin, sem)

    @pl.when(x == 0)
    def _():
        wait_for(din.at[pl.ds(0, 3)], din_recv)
        part[...] = decode(din[1]) + decode(din[2]) + decode(din[3])

    seven_or_eight(y_recv)

    @pl.when(x != 0)
    def _():
        wait_for(din.at[0], din_recv)
        part[...] = decode(din[0])

    total = part[...]
    for i in range(8):
        total = total + decode(yin[i])

    master = state[0]
    new_moment = 0.9 * state[1] + 0.1 * total
    new_second = 0.95 * state[2] + 0.05 * total * total
    update = new_moment / first_fix / (jnp.sqrt(new_second / second_fix) + 1e-08) + 0.1 * master
    new_master = master - 0.03 * update

    def row_of(yy, xx, cc):
        return lax.rem(yy, 2) * 32 + (yy // 2) * 8 + xx * 2 + cc

    slot = {d: i for i, d in enumerate((1, 2, 3, 4, 5, 6, 7))}
    COLUMN, GROUP, OPPOSITE, BESIDE, CORNER, SIBLING = 0, 7, 14, 15, 16, 17
    NEAR = (1, 7, 2, 6)

    def at_y(d):
        return lax.rem(y + d, 8)

    def pass_on(r, index, where):
        remote(rows.at[r], rows.at[r], sent.at[3], a_recv.at[index], where).start()

    def arrived(n, index):
        wait_for(rows.at[pl.ds(0, n)], a_recv.at[index])

    me = row_of(y, x, c)
    rows[me] = new_master.astype(BF16)
    for d in Y_ORDER:
        pass_on(me, COLUMN + slot[8 - d], dev(at_y(d), x, c))
    pass_on(me, OPPOSITE, across[0])
    pass_on(me, BESIDE, across[1])
    pass_on(me, BESIDE, across[2])
    pass_on(me, SIBLING, sibling)

    def column(d):
        arrived(1, COLUMN + slot[d])
        r = row_of(at_y(d), x, c)
        if d not in NEAR:
            pass_on(r, GROUP + slot[d], across[0])
        pass_on(r, GROUP + slot[d], across[1])
        pass_on(r, GROUP + slot[d], across[2])
        pass_on(r, SIBLING, sibling)

    def opposite():
        arrived(1, OPPOSITE)
        r = row_of(y, xo, c)
        for d in NEAR:
            pass_on(r, CORNER, dev(at_y(d), x, c))
        pass_on(r, SIBLING, sibling)

    def group(d):
        arrived(2 if d in NEAR else 3, GROUP + slot[d])
        pass_on(row_of(at_y(d), xp, c), SIBLING, sibling)
        pass_on(row_of(at_y(d), xm, c), SIBLING, sibling)
        if d not in NEAR:
            pass_on(row_of(at_y(d), xo, c), SIBLING, sibling)

    def beside():
        arrived(2, BESIDE)
        pass_on(row_of(y, xp, c), SIBLING, sibling)
        pass_on(row_of(y, xm, c), SIBLING, sibling)

    def corner():
        arrived(4, CORNER)
        for d in NEAR:
            pass_on(row_of(at_y(d), xo, c), SIBLING, sibling)

    steps = {"o": opposite, "b": beside, "k": corner}
    for what in A_ORDER:
        if what in steps:
            steps[what]()
        elif what[0] == "c":
            column(int(what[1]))
        else:
            group(int(what[1]))
    new_master_ref[...] = new_master
    new_moment_ref[...] = new_moment
    new_second_ref[...] = new_second
    arrived(32, SIBLING)

    for gp in range(4):
        for s in range(16):
            wide[gp % 2, s] = rows[gp * 16 + s].astype(F32)
        w = wide.at[gp % 2].reshape(16 * J, 128)
        for j in range(J):
            tiles[pl.ds(gp * 16, 16), pl.ds(j * 128, 128)] = w[pl.ds(j, 16, stride=J), :].astype(BF16)

    wait_for(sib, sent.at[0])
    wait_for(xcode, sent.at[1])
    seven_or_eight(sent.at[2])
    wait_for(rows.at[pl.ds(0, 63)], sent.at[3])


def write_out(m_ref, v_ref, s_ref, p_ref, m_out, v_out, s_out, p_out, sems):
    copies = [
        pltpu.make_async_copy(src, dst, sems.at[i])
        for i, (src, dst) in enumerate(((p_ref, p_out), (m_ref, m_out), (v_ref, v_out), (s_ref, s_out)))
    ]
    for cp in copies:
        cp.start()
    for cp in copies:
        cp.wait()


def per_device(grads, master, moment, second, step):
    g = grads.reshape(8, 8, J, 128).transpose(0, 2, 1, 3)
    row = jax.ShapeDtypeStruct((J, 128), F32)
    vmem = pl.BlockSpec(memory_space=pltpu.VMEM)
    hbm = pl.BlockSpec(memory_space=pltpu.HBM)
    dma = pltpu.SemaphoreType.DMA
    parts = pl.pallas_call(
        reduce_update_gather,
        out_shape=(row, row, row, jax.ShapeDtypeStruct((64, J * 128), BF16)),
        in_specs=[pl.BlockSpec(memory_space=pltpu.SMEM)] + [hbm] * 4,
        out_specs=(vmem,) * 4,
        scratch_shapes=[
            pltpu.VMEM((64, J, 128), BF16),
            pltpu.VMEM((2, 16, J, 128), F32),
            pltpu.VMEM((4, J, 8, 128), F32),
            pltpu.VMEM((4, J, 8, 128), F32),
            pltpu.VMEM((4, 2, J, 128), F32),
            pltpu.VMEM((4, 3, 2, CODE, 128), I16),
            pltpu.VMEM((4, 3, 2, CODE, 128), I16),
            pltpu.VMEM((4, 2, CODE, 128), I16),
            pltpu.VMEM((8, CODE, 128), I16),
            pltpu.VMEM((4, CODE, 128), I16),
            pltpu.VMEM((J, 128), F32),
            pltpu.VMEM((3, J, 128), F32),
            dma((4,)), dma, dma((4,)), dma((4,)), dma((4,)), dma, dma, dma((18,)),
            pltpu.SemaphoreType.REGULAR((4,)), pltpu.SemaphoreType.REGULAR((4,)),
        ],
        compiler_params=pltpu.CompilerParams(
            collective_id=0, has_side_effects=True, vmem_limit_bytes=24 << 20
        ),
    )(step, *[
        pltpu.with_memory_space_constraint(a, pltpu.HBM)
        for a in (g, master.reshape(J, 128), moment.reshape(J, 128), second.reshape(J, 128))
    ])
    new_master, new_moment, new_second, params = pl.pallas_call(
        write_out,
        out_shape=(row, row, row, jax.ShapeDtypeStruct((64, J * 128), BF16)),
        in_specs=[vmem] * 4,
        out_specs=(hbm,) * 4,
        scratch_shapes=[
            dma((4,)),
        ],
        compiler_params=pltpu.CompilerParams(vmem_limit_bytes=24 << 20),
    )(*parts)
    flat = (1, J * 128)
    return (new_master.reshape(flat), new_moment.reshape(flat), new_second.reshape(flat), params)


def solution(mesh):
    placed = (
        P(("section", "pair"), "dp", None, None),
        P(("section", "pair", "dp"), None),
        P(("section", "pair", "dp"), None),
        P(("section", "pair", "dp"), None),
        P("section"),
    )
    return jax.shard_map(
        per_device,
        mesh=mesh,
        in_specs=placed,
        out_specs=(
            P(("section", "pair", "dp"), None),
            P(("section", "pair", "dp"), None),
            P(("section", "pair", "dp"), None),
            P("section", None),
        ),
        check_vma=False,
    )
```

```python
import jax
import jax.numpy as jnp
from jax import lax
from jax.experimental import pallas as pl
from jax.experimental.pallas import tpu as pltpu
from jax.sharding import PartitionSpec as P

MESH = pl.DeviceIdType.MESH
F32 = jnp.float32
BF16 = jnp.bfloat16
I16 = jnp.int16
J = 56
CODE = 64
TOP = 32700.0
STEPS = 256.0
FAR = (1, 7, 2, 6, 3, 5, 4)
Y_ORDER = (1, 7, 4, 2, 6, 3, 5)
A_ORDER = ("c1", "c7", "o", "c2", "c6", "c3", "c5", "c4", "b", "g1", "g7", "g2", "g6", "k", "g3", "g5", "g4")


def encode(v):
    v = v.reshape(7, 8, 128)
    largest = jnp.maximum(jnp.max(jnp.abs(v), axis=0), 1e-30)
    e = jnp.ceil(jnp.log2(largest) * STEPS)
    q = jnp.round(v * (TOP * jnp.exp2(e * (-1.0 / STEPS)))[None])
    return jnp.concatenate([q.reshape(J, 128), e], axis=0).astype(jnp.int32).astype(I16)


def decode(code):
    f = code.astype(jnp.int32).astype(F32)
    scale = jnp.exp2(f[J:] * (1.0 / STEPS)) * (1.0 / TOP)
    return (f[:J].reshape(7, 8, 128) * scale[None]).reshape(J, 128)


def reduce_update_gather(
    step_ref, g_ref, master_hbm, moment_hbm, second_hbm,
    new_master_ref, new_moment_ref, new_second_ref, tiles,
    rows, wide, mine, sib, xs, xcode, xin, ycode, yin, din, part, state,
    load_sem, state_sem, sent, d_recv, x_recv, y_recv, din_recv, a_recv, ready, told,
):
    ylo = lax.axis_index("pair")
    dp = lax.axis_index("dp")
    c = lax.rem(dp, 2)
    x = lax.rem(dp // 2, 4)
    yhi = dp // 8
    y = yhi * 2 + ylo
    oc = 1 - c
    xp = lax.rem(x + 1, 4)
    xm = lax.rem(x + 3, 4)
    xo = lax.rem(x + 2, 4)

    def dev(yy, xx, cc):
        return {"pair": lax.rem(yy, 2), "dp": ((yy // 2) * 4 + xx) * 2 + cc}

    sibling = dev(y, x, oc)
    across = [dev(y, xx, c) for xx in (xo, xp, xm)]

    def remote(src, dst, ssem, rsem, where):
        return pltpu.make_async_remote_copy(
            src_ref=src, dst_ref=dst, send_sem=ssem, recv_sem=rsem,
            device_id=where, device_id_type=MESH,
        )

    def wait_for(ref, sem):
        pltpu.make_async_copy(ref, ref, sem).wait()

    both, either = jnp.logical_and, jnp.logical_or
    base = y == 0
    first = both(base, x == 0)
    mate = both(base, x != 0)
    above = both(x == 0, y != 0)
    direct = [both(base, either(x == 0, xx == 0)) for xx in (xo, xp, xm)]

    column_of = [dev(lax.rem(y + d, 8), x, 1) for d in FAR]
    row_mates = [dev(y, xx, 1) for xx in (xo, xp, xm)]

    def signal(sem, where):
        pl.semaphore_signal(sem, inc=1, device_id=where, device_id_type=MESH)

    barrier = pltpu.get_barrier_semaphore()
    signal(barrier, sibling)

    @pl.when(c == 1)
    def _():
        for where in row_mates + column_of:
            signal(barrier, where)

    hi_of = [lax.rem(yhi + d, 4) for d in (2, 3, 1, 0)]
    for k in range(4):
        pltpu.make_async_copy(g_ref.at[c * 4 + hi_of[k]], mine.at[k], load_sem.at[k]).start()
    for i, src in enumerate((master_hbm, moment_hbm, second_hbm)):
        pltpu.make_async_copy(src, state.at[i], state_sem).start()

    @pl.when(c == 1)
    def _():
        pl.semaphore_wait(barrier, 11)

    @pl.when(c == 0)
    def _():
        pl.semaphore_wait(barrier, 1)

    for k in range(4):
        remote(g_ref.at[oc * 4 + hi_of[k]], sib.at[k], sent.at[0], d_recv.at[k], sibling).start()

    @pl.when(c == 1)
    def _():
        for where in row_mates:
            signal(ready.at[first.astype(jnp.int32)], where)
        for where in column_of:
            signal(ready.at[2 - first.astype(jnp.int32)], where)

        @pl.when(mate)
        def _():
            pl.semaphore_wait(ready.at[0], 2)

        @pl.when(jnp.logical_not(mate))
        def _():
            pl.semaphore_wait(ready.at[0], 3)

        @pl.when(base)
        def _():
            pl.semaphore_wait(ready.at[3], 7)

        @pl.when(jnp.logical_not(base))
        def _():
            signal(ready.at[3], dev(0, x, 1))

        signal(told.at[0], sibling)

    def send_direct(k, i, xx):
        for cc in range(2):
            remote(
                xcode.at[k, i, cc], din.at[x], sent.at[1], din_recv, dev(hi_of[k] * 2 + c, xx, cc)
            ).start()

    def send_x(k, i):
        remote(xcode.at[k, i], xin.at[k, i], sent.at[1], x_recv.at[k], across[i]).start()

    def stage_sum(k):
        wait_for(mine.at[k], load_sem.at[k])
        wait_for(sib.at[k], d_recv.at[k])
        a = mine.at[k].reshape(J * 8, 128)
        b = sib.at[k].reshape(J * 8, 128)

        def summed(xx, cc):
            pieces = []
            for jb in range(7):
                sl = pl.ds(jb * 64 + xx * 2 + cc, 8, stride=8)
                pieces.append(a[sl, :] + b[sl, :])
            return jnp.concatenate(pieces, axis=0)

        for i, xx in enumerate((xo, xp, xm)):
            for cc in range(2):
                xcode[k, i, cc] = encode(summed(xx, cc))

            if k == 0 and i == 0:
                @pl.when(c == 0)
                def _():
                    pl.semaphore_wait(told.at[0], 1)

            now = direct[i]
            if k == 3:
                now = both(now, jnp.logical_not(both(xx == 0, hi_of[k] * 2 + c == 0)))

            @pl.when(now)
            def _(i=i, xx=xx):
                send_direct(k, i, xx)

            @pl.when(jnp.logical_not(direct[i]))
            def _(i=i):
                send_x(k, i)

        for cc in range(2):
            xs[k, cc] = summed(x, cc)

    def stage_y(k):
        yy = hi_of[k] * 2 + c
        @pl.when(jnp.logical_not(base))
        def _():
            wait_for(xin.at[k], x_recv.at[k])

        @pl.when(mate)
        def _():
            wait_for(xin.at[k, pl.ds(0, 2)], x_recv.at[k])

        for i, sender in enumerate((0, 2, 1)):
            @pl.when(jnp.logical_not(direct[sender]))
            def _(i=i):
                for cc in range(2):
                    xs[k, cc] = xs[k, cc] + decode(xin[k, i, cc])

        for cc in range(2):
            ycode[k, cc] = encode(xs[k, cc])

        if k == 3:
            for cc in range(2):
                own = both(c == ylo, c == cc)

                @pl.when(own)
                def _(cc=cc):
                    yin[y] = ycode[k, cc]

                @pl.when(jnp.logical_not(either(own, both(above, yy == 0))))
                def _(cc=cc):
                    send_y(k, cc)
        else:
            @pl.when(jnp.logical_not(both(above, yy == 0)))
            def _():
                for cc in range(2):
                    send_y(k, cc)

    def send_y(k, cc):
        remote(
            ycode.at[k, cc], yin.at[y], sent.at[2], y_recv, dev(hi_of[k] * 2 + c, x, cc)
        ).start()

    stage_sum(0)
    stage_sum(1)
    stage_sum(2)
    stage_sum(3)

    @pl.when(c == 1)
    def _():
        @pl.when(above)
        def _():
            pl.semaphore_wait(ready.at[2], 6)

        @pl.when(jnp.logical_not(above))
        def _():
            pl.semaphore_wait(ready.at[2], 7)

        signal(told.at[2], sibling)

    wait_for(state, state_sem)
    t = step_ref[0]
    p1 = jnp.float32(1.0)
    p2 = jnp.float32(1.0)
    b1, b2 = 0.9, 0.95
    for bit in range(8):
        on = lax.rem(lax.shift_right_logical(t, bit), 2) == 1
        p1 = p1 * jnp.where(on, jnp.float32(b1), jnp.float32(1.0))
        p2 = p2 * jnp.where(on, jnp.float32(b2), jnp.float32(1.0))
        b1, b2 = b1 * b1, b2 * b2
    first_fix = jnp.full((J, 128), 1.0 - p1, F32)
    second_fix = jnp.full((J, 128), 1.0 - p2, F32)

    @pl.when(c == 0)
    def _():
        pl.semaphore_wait(told.at[2], 1)

    stage_y(0)
    stage_y(1)
    stage_y(2)
    stage_y(3)

    @pl.when(either(mate, above))
    def _():
        @pl.when(c == 1)
        def _():
            pl.semaphore_wait(ready.at[1], 1)
            signal(told.at[1], sibling)

        @pl.when(c == 0)
        def _():
            pl.semaphore_wait(told.at[1], 1)
            for i, xx in enumerate((xo, xp, xm)):
                @pl.when(both(mate, xx == 0))
                def _(i=i, xx=xx):
                    send_direct(3, i, xx)

            for k in range(4):
                @pl.when(both(above, hi_of[k] == 0))
                def _(k=k):
                    for cc in range(2):
                        send_y(k, cc)

    def seven_or_eight(sem):
        @pl.when(c == ylo)
        def _():
            wait_for(yin.at[pl.ds(0, 7)], sem)

        @pl.when(c != ylo)
        def _():
            wait_for(yin, sem)

    @pl.when(x == 0)
    def _():
        wait_for(din.at[pl.ds(0, 3)], din_recv)
        part[...] = decode(din[1]) + decode(din[2]) + decode(din[3])

    seven_or_eight(y_recv)

    @pl.when(x != 0)
    def _():
        wait_for(din.at[0], din_recv)
        part[...] = decode(din[0])

    total = part[...]
    for i in range(8):
        total = total + decode(yin[i])

    master = state[0]
    new_moment = 0.9 * state[1] + 0.1 * total
    new_second = 0.95 * state[2] + 0.05 * total * total
    update = new_moment / first_fix / (jnp.sqrt(new_second / second_fix) + 1e-08) + 0.1 * master
    new_master = master - 0.03 * update

    def row_of(yy, xx, cc):
        return lax.rem(yy, 2) * 32 + (yy // 2) * 8 + xx * 2 + cc

    slot = {d: i for i, d in enumerate((1, 2, 3, 4, 5, 6, 7))}
    COLUMN, GROUP, OPPOSITE, BESIDE, CORNER, SIBLING = 0, 7, 14, 15, 16, 17
    NEAR = (1, 7, 2, 6)

    def at_y(d):
        return lax.rem(y + d, 8)

    def pass_on(r, index, where):
        remote(rows.at[r], rows.at[r], sent.at[3], a_recv.at[index], where).start()

    def arrived(n, index):
        wait_for(rows.at[pl.ds(0, n)], a_recv.at[index])

    me = row_of(y, x, c)
    rows[me] = new_master.astype(BF16)
    for d in Y_ORDER:
        pass_on(me, COLUMN + slot[8 - d], dev(at_y(d), x, c))
    pass_on(me, OPPOSITE, across[0])
    pass_on(me, BESIDE, across[1])
    pass_on(me, BESIDE, across[2])
    pass_on(me, SIBLING, sibling)

    def column(d):
        arrived(1, COLUMN + slot[d])
        r = row_of(at_y(d), x, c)
        if d not in NEAR:
            pass_on(r, GROUP + slot[d], across[0])
        pass_on(r, GROUP + slot[d], across[1])
        pass_on(r, GROUP + slot[d], across[2])
        pass_on(r, SIBLING, sibling)

    def opposite():
        arrived(1, OPPOSITE)
        r = row_of(y, xo, c)
        for d in NEAR:
            pass_on(r, CORNER, dev(at_y(d), x, c))
        pass_on(r, SIBLING, sibling)

    def group(d):
        arrived(2 if d in NEAR else 3, GROUP + slot[d])
        pass_on(row_of(at_y(d), xp, c), SIBLING, sibling)
        pass_on(row_of(at_y(d), xm, c), SIBLING, sibling)
        if d not in NEAR:
            pass_on(row_of(at_y(d), xo, c), SIBLING, sibling)

    def beside():
        arrived(2, BESIDE)
        pass_on(row_of(y, xp, c), SIBLING, sibling)
        pass_on(row_of(y, xm, c), SIBLING, sibling)

    def corner():
        arrived(4, CORNER)
        for d in NEAR:
            pass_on(row_of(at_y(d), xo, c), SIBLING, sibling)

    steps = {"o": opposite, "b": beside, "k": corner}
    for what in A_ORDER:
        if what in steps:
            steps[what]()
        elif what[0] == "c":
            column(int(what[1]))
        else:
            group(int(what[1]))
    new_master_ref[...] = new_master
    new_moment_ref[...] = new_moment
    new_second_ref[...] = new_second
    arrived(32, SIBLING)

    for gp in range(4):
        for s in range(16):
            wide[gp % 2, s] = rows[gp * 16 + s].astype(F32)
        w = wide.at[gp % 2].reshape(16 * J, 128)
        for j in range(J):
            tiles[pl.ds(gp * 16, 16), pl.ds(j * 128, 128)] = w[pl.ds(j, 16, stride=J), :].astype(BF16)

    wait_for(sib, sent.at[0])
    wait_for(xcode, sent.at[1])
    seven_or_eight(sent.at[2])
    wait_for(rows.at[pl.ds(0, 63)], sent.at[3])


def write_out(m_ref, v_ref, s_ref, p_ref, m_out, v_out, s_out, p_out, sems):
    copies = [
        pltpu.make_async_copy(src, dst, sems.at[i])
        for i, (src, dst) in enumerate(((p_ref, p_out), (m_ref, m_out), (v_ref, v_out), (s_ref, s_out)))
    ]
    for cp in copies:
        cp.start()
    for cp in copies:
        cp.wait()


def per_device(grads, master, moment, second, step):
    g = grads.reshape(8, 8, J, 128).transpose(0, 2, 1, 3)
    row = jax.ShapeDtypeStruct((J, 128), F32)
    vmem = pl.BlockSpec(memory_space=pltpu.VMEM)
    hbm = pl.BlockSpec(memory_space=pltpu.HBM)
    dma = pltpu.SemaphoreType.DMA
    parts = pl.pallas_call(
        reduce_update_gather,
        out_shape=(row, row, row, jax.ShapeDtypeStruct((64, J * 128), BF16)),
        in_specs=[pl.BlockSpec(memory_space=pltpu.SMEM)] + [hbm] * 4,
        out_specs=(vmem,) * 4,
        scratch_shapes=[
            pltpu.VMEM((64, J, 128), BF16),
            pltpu.VMEM((2, 16, J, 128), F32),
            pltpu.VMEM((4, J, 8, 128), F32),
            pltpu.VMEM((4, J, 8, 128), F32),
            pltpu.VMEM((4, 2, J, 128), F32),
            pltpu.VMEM((4, 3, 2, CODE, 128), I16),
            pltpu.VMEM((4, 3, 2, CODE, 128), I16),
            pltpu.VMEM((4, 2, CODE, 128), I16),
            pltpu.VMEM((8, CODE, 128), I16),
            pltpu.VMEM((4, CODE, 128), I16),
            pltpu.VMEM((J, 128), F32),
            pltpu.VMEM((3, J, 128), F32),
            dma((4,)), dma, dma((4,)), dma((4,)), dma((4,)), dma, dma, dma((18,)),
            pltpu.SemaphoreType.REGULAR((4,)), pltpu.SemaphoreType.REGULAR((4,)),
        ],
        compiler_params=pltpu.CompilerParams(
            collective_id=0, has_side_effects=True, vmem_limit_bytes=24 << 20
        ),
    )(step, *[
        pltpu.with_memory_space_constraint(a, pltpu.HBM)
        for a in (g, master.reshape(J, 128), moment.reshape(J, 128), second.reshape(J, 128))
    ])
    new_master, new_moment, new_second, params = pl.pallas_call(
        write_out,
        out_shape=(row, row, row, jax.ShapeDtypeStruct((64, J * 128), BF16)),
        in_specs=[vmem] * 4,
        out_specs=(hbm,) * 4,
        scratch_shapes=[
            dma((4,)),
        ],
        compiler_params=pltpu.CompilerParams(vmem_limit_bytes=24 << 20),
    )(*parts)
    flat = (1, J * 128)
    return (new_master.reshape(flat), new_moment.reshape(flat), new_second.reshape(flat), params)


def solution(mesh):
    placed = (
        P(("section", "pair"), "dp", None, None),
        P(("section", "pair", "dp"), None),
        P(("section", "pair", "dp"), None),
        P(("section", "pair", "dp"), None),
        P("section"),
    )
    return jax.shard_map(
        per_device,
        mesh=mesh,
        in_specs=placed,
        out_specs=(
            P(("section", "pair", "dp"), None),
            P(("section", "pair", "dp"), None),
            P(("section", "pair", "dp"), None),
            P("section", None),
        ),
        check_vma=False,
    )
```
